32 devices in a mesh: groups: 2 (over x), row: 16 (over z, y, core).
Axes of the slice: x: 2, y: 2, z: 4, core: 2. Of those that a mesh axis runs over, the one named last changes fastest.
Arguments:
- panels: float32 [53248, 768], P(('groups', 'row')), parts along dimension 0, as said below
- weights: float32 [53248, 1792], P(('groups', 'row')), parts along dimension 0, may hold values from -6 to 6
- block_ids: int32 [6], P('groups'), parts along dimension 0, may hold values from 0 to 103, as said below
Outputs:
- pruned_weights: float32 [53248, 1792], P(('groups', 'row')), parts along dimension 0
- losses: float32 [6], P('groups'), parts along dimension 0
The draws below stay inside these ranges and needn't reach their ends.
There are 2 independent parts, one for each index of `groups`. The reference program is written for one: setup_inputs(seed, part) draws one part's arguments, and reference() takes and returns one part's arrays. A program takes and returns all parts, laid end to end along the dimension named above; each array names one. Nothing has to cross between parts.
Inputs may be any that keep to these rules, and one draw needn't show every extreme that they name: `panels`: the columns, at the listed blocks' hidden units and in pick order, of a symmetric positive definite matrix of order 26624. `block_ids`: 3 distinct block numbers; the first and the last block of the window are always among them.
All inputs are finite; a program needn't handle non-finite values.
Results may differ from the reference program's by a relative error of at most 0.00017.
Values sent between devices are 32-bit elements; how exact they have to be, the bound alone decides.
No kernel may reach another device: no remote copies, remote signals or barrier semaphores. Data moves between devices by JAX's collectives and lax.ppermute only.
A program may use at most 128 MiB of HBM per device.

```python
import jax
import jax.numpy as jnp
from jax import lax

ORDER = 26624
COLS = 1792
BLOCK = 256
PICKS = 3


def chosen_blocks(key):
    block_count = ORDER // BLOCK
    middle = 1 + jax.random.permutation(jax.random.fold_in(key, 7), block_count - 2)[:PICKS - 2]
    ends = jnp.array([0, block_count - 1], dtype=jnp.int32)
    listed = jnp.concatenate([ends, middle.astype(jnp.int32)])
    shuffle = jax.random.permutation(jax.random.fold_in(key, 13), PICKS)
    return listed[shuffle].astype(jnp.int32)


def draw_block_ids(key, part):
    return chosen_blocks(key)


def draw_panels(key, part):
    block_list = chosen_blocks(key)
    columns = (block_list[:, None] * BLOCK + jnp.arange(BLOCK, dtype=jnp.int32)[None, :]).reshape(-1)
    keys = jax.random.split(jax.random.fold_in(key, 11), 2)
    inner = 4 * BLOCK
    factors = jax.random.normal(keys[0], (ORDER, inner), jnp.float32)
    diagonal = jnp.exp(jax.random.uniform(keys[1], (ORDER,), jnp.float32, jnp.log(0.5), jnp.log(2.0)))
    picked = factors[columns]
    matrix = jnp.dot(factors, picked.T, precision=lax.Precision.HIGHEST) / inner
    all_rows = jnp.arange(ORDER, dtype=jnp.int32)
    matrix = matrix + jnp.where(all_rows[:, None] == columns[None, :], diagonal[:, None], 0.0)
    return matrix.astype(jnp.float32)


def levels(key, shape, cuts, low, high):
    factor_of, own = 1.0, jax.random.fold_in(key, 6)
    for position, shards_of in cuts:
        steps = jnp.exp(jax.random.uniform(jax.random.fold_in(own, position), (shards_of,), jnp.float32, low / len(cuts), high / len(cuts)))
        factor_of = factor_of * jnp.repeat(steps, shape[position] // shards_of).reshape([-1 if axis == position else 1 for axis in range(len(shape))])
    return factor_of


def normal_values(own_key, shape, scale, reach, cuts=(), kind=jnp.bfloat16):
    entries = jax.random.normal(own_key, shape, jnp.float32) * scale
    if len(cuts) > 0:
        entries = levels(own_key, shape, cuts, -0.22, 0.18) * entries
    return jnp.clip(entries, min=-reach, max=reach).astype(kind)


def setup_inputs(seed: int = 0, part: int = 0) -> dict:
    arg_keys = jax.random.split(jax.random.key(seed), 4)
    own_keys = jax.random.split(jax.random.fold_in(arg_keys[3], part), 4)
    return {
        "panels": draw_panels(jax.random.fold_in(jax.random.fold_in(arg_keys[3], part), 71), part),
        "weights": normal_values(own_keys[1], (ORDER, COLS), 1.0, 6.0, ((0, 16),), jnp.float32),
        "block_ids": draw_block_ids(jax.random.fold_in(jax.random.fold_in(arg_keys[3], part), 71), part),
    }


exact_mode = lax.Precision.HIGHEST

def chol_solve(factor, rhs):
    middle = lax.linalg.triangular_solve(factor, rhs, left_side=True, lower=True)
    return lax.linalg.triangular_solve(factor, middle, left_side=True, lower=True, transpose_a=True)

def reference(panels, weights, block_ids):
    current_panels = panels
    current = weights
    losses = []
    all_rows = jnp.arange(ORDER, dtype=jnp.int32)
    zero_index = jnp.zeros((), jnp.int32)
    for number in range(PICKS):
        start_row = (block_ids[number] * BLOCK).astype(jnp.int32)
        low_edge = number * BLOCK
        row_block = lax.dynamic_slice(current_panels, (start_row, zero_index), (BLOCK, PICKS * BLOCK))
        diag_block = row_block[:, low_edge:low_edge + BLOCK]
        col_panel = current_panels[:, low_edge:low_edge + BLOCK]
        chosen = lax.dynamic_slice(current, (start_row, zero_index), (BLOCK, COLS))
        factor = jnp.linalg.cholesky(diag_block)
        solved = chol_solve(factor, chosen)
        losses.append(jnp.sum(chosen * solved) / (2.0 * BLOCK * COLS))
        current = current - jnp.dot(col_panel, solved, precision=exact_mode)
        inside = (all_rows >= start_row) & (all_rows < start_row + BLOCK)
        current = jnp.where(inside[:, None], jnp.zeros_like(current), current)
        if number < PICKS - 1:
            left_factor = chol_solve(factor, col_panel.T).T
            current_panels = current_panels - jnp.dot(left_factor, row_block, precision=exact_mode)
    return (current, jnp.stack(losses))
```

```python
import functools

import jax
import jax.numpy as jnp
from jax import lax
from jax.experimental import pallas as pl
from jax.experimental.pallas import tpu as pltpu
from jax.sharding import PartitionSpec as P

BLOCK = 256
PICKS = 3
HALF = BLOCK // 2
SUB = 8
LANES = 128
EXACT = lax.Precision.HIGHEST
F32 = jnp.float32
BF16 = jnp.bfloat16


def mm(a, b):
    return lax.dot_general(a, b, (((1,), (0,)), ((), ())), precision=EXACT, preferred_element_type=F32)


def mm_nt(a, b):
    return lax.dot_general(a, b, (((1,), (1,)), ((), ())), precision=EXACT, preferred_element_type=F32)


def mm_tn(a, b):
    return lax.dot_general(a, b, (((0,), (0,)), ((), ())), precision=EXACT, preferred_element_type=F32)


def lane_bcast(x, c):
    return jnp.broadcast_to(x[:, c : c + 1], (SUB, LANES))


def row_bcast(x, j):
    return jnp.broadcast_to(x[j : j + 1, :], (SUB, LANES))


def inv_half(m):
    n_panels = HALF // SUB
    rows = [m[SUB * i : SUB * i + SUB, :] for i in range(n_panels)]
    lane = lax.broadcasted_iota(jnp.int32, (SUB, LANES), 1)
    sub = lax.broadcasted_iota(jnp.int32, (SUB, LANES), 0)
    for p in range(n_panels):
        panel = rows[p]
        cols = [lane_bcast(panel, SUB * p + k) for k in range(SUB)]
        for j in range(SUB):
            is_j = sub == j
            r = 1.0 / row_bcast(cols[j], j)
            f = cols[j] * r
            panel = jnp.where(lane == SUB * p + j, jnp.where(is_j, 1.0, 0.0), panel)
            u = row_bcast(panel, j)
            panel = jnp.where(is_j, u * r, panel - f * u)
            for k in range(j + 1, SUB):
                uk = row_bcast(cols[k], j)
                cols[k] = jnp.where(is_j, uk * r, cols[k] - f * uk)
        reps = [row_bcast(panel, k) for k in range(SUB)]
        in_panel = (lane >= SUB * p) & (lane < SUB * p + SUB)
        for step in range(1, n_panels):
            i = (p + step) % n_panels
            t = [lane_bcast(rows[i], SUB * p + k) * reps[k] for k in range(SUB)]
            total = ((t[0] + t[1]) + (t[2] + t[3])) + ((t[4] + t[5]) + (t[6] + t[7]))
            rows[i] = jnp.where(in_panel, 0.0, rows[i]) - total
        rows[p] = panel
    return jnp.concatenate(rows, axis=0)


def inv_block(b):
    c = b[HALF:, :HALF]
    ai = inv_half(b[:HALF, :HALF])
    g = mm(c, ai)
    si = inv_half(b[HALF:, HALF:] - mm_nt(g, c))
    h = mm(si, g)
    top = jnp.concatenate([ai + mm_tn(g, h), -h.T], axis=1)
    return jnp.concatenate([top, jnp.concatenate([-h, si], axis=1)], axis=0)


def split(x):
    hi = x.astype(BF16)
    return hi, (x - hi.astype(F32)).astype(BF16)


def dot3(ah, al, bh, bl):
    d = lambda x, y: jnp.dot(x, y, preferred_element_type=F32)
    return d(ah, bh) + (d(ah, bl) + d(al, bh))


def first_kernel(sc, mine, other, s_out, g_out, a_out, fl, mid, blk):
    core, chip, c_f, c_l, c_m = sc[0], sc[1], sc[2], sc[3], sc[4]
    n_chip, s = mine.shape[0], mine.shape[1]
    width = PICKS * BLOCK
    for k in range(n_chip):
        row = pl.multiple_of((chip ^ k) * s, SUB)
        fl[core, pl.ds(row, s), :] = mine[k, :, :width]
        mid[core, pl.ds(row, s), :] = mine[k, :, width:]
        fl[1 - core, pl.ds(row, s), :] = other[k, :, :width]
        mid[1 - core, pl.ds(row, s), :] = other[k, :, width:]
    for j in range(PICKS):
        blk[c_f, j] = fl[0, :, j * BLOCK : (j + 1) * BLOCK]
        blk[c_l, j] = fl[1, :, j * BLOCK : (j + 1) * BLOCK]
    blk[c_m, c_f] = blk[c_f, c_m].T
    blk[c_m, c_l] = blk[c_l, c_m].T
    blk[c_m, c_m, :, :HALF] = mid[0]
    blk[c_m, c_m, :, HALF:] = mid[1]
    s0 = inv_block(blk[0, 0])
    s_out[...] = s0
    a10, a20 = blk[1, 0], blk[2, 0]
    g10, g20 = mm(a10, s0), mm(a20, s0)
    g_out[0] = g10
    g_out[1] = g20
    a_out[0] = blk[1, 1] - mm_nt(g10, a10)
    a_out[1] = blk[2, 1] - mm_nt(g20, a10)
    a_out[2] = blk[2, 2] - mm_nt(g20, a20)


def second_kernel(a_in, s_out, g_out, a_out):
    s1 = inv_block(a_in[0])
    s_out[...] = s1
    a21 = a_in[1]
    g21 = mm(a21, s1)
    g_out[...] = g21
    a_out[...] = a_in[2] - mm_nt(g21, a21)


def third_kernel(a_in, s0, s1, g, g21, s_out, k_out):
    s2 = inv_block(a_in[...])
    s_out[...] = s2
    g10, g20 = g[0], g[1]
    j21 = -g21[...]
    j20 = mm(g21[...], g10) - g20
    k21, k20 = mm(s2, j21), mm(s2, j20)
    t10 = mm(s1[...], g10)
    k11 = s1[...] + mm_tn(j21, k21)
    k10 = mm_tn(j21, k20) - t10
    k00 = s0[...] + mm_tn(g10, t10) + mm_tn(j20, k20)
    e = lambda i: slice(i * BLOCK, (i + 1) * BLOCK)
    k_out[e(2), e(2)] = s2
    k_out[e(2), e(1)] = k21
    k_out[e(1), e(2)] = k21.T
    k_out[e(2), e(0)] = k20
    k_out[e(0), e(2)] = k20.T
    k_out[e(1), e(1)] = k11
    k_out[e(1), e(0)] = k10
    k_out[e(0), e(1)] = k10.T
    k_out[e(0), e(0)] = k00


def left_kernel(k_ref, p_ref, hi_out, lo_out, kh, kl):
    @pl.when(pl.program_id(0) == 0)
    def _():
        kh[...], kl[...] = split(k_ref[...])

    ph, pw = split(p_ref[...])
    hi_out[...], lo_out[...] = split(dot3(ph, pw, kh[...], kl[...]))


def final_kernel(sc, w_ref, th, tl, fl_mine, fl_other, m_mine, m_other, s0, s1, s2, g, g21, o_ref, loss, ws, wh, wl, sems):
    core, chip, c_f, c_l, c_m, first = sc[0], sc[1], sc[2], sc[3], sc[4], sc[5]
    tile, cols = o_ref.shape
    n_chip, s = fl_mine.shape[0], fl_mine.shape[1]

    @pl.when(pl.program_id(0) == 0)
    def _():
        copies = []
        half_cols = cols // 2
        mine_at = jnp.where(core == 0, c_f, c_l) * BLOCK
        other_at = jnp.where(core == 0, c_l, c_f) * BLOCK
        mine_col = pl.multiple_of(core * half_cols, LANES)
        other_col = pl.multiple_of((1 - core) * half_cols, LANES)
        for k in range(n_chip):
            row = (chip ^ k) * s
            at = lambda base: pl.ds(pl.multiple_of(base + row, SUB), s)
            copies.append(pltpu.make_async_copy(fl_mine.at[k], ws.at[at(mine_at), :], sems.at[k, 0]))
            copies.append(pltpu.make_async_copy(fl_other.at[k], ws.at[at(other_at), :], sems.at[k, 1]))
            copies.append(pltpu.make_async_copy(m_mine.at[k], ws.at[at(c_m * BLOCK), pl.ds(mine_col, half_cols)], sems.at[k, 2]))
            copies.append(pltpu.make_async_copy(m_other.at[k], ws.at[at(c_m * BLOCK), pl.ds(other_col, half_cols)], sems.at[k, 3]))
        for c in copies:
            c.start()
        for c in copies:
            c.wait()
        wh[...], wl[...] = split(ws[...])
        e = lambda i: slice(i * BLOCK, (i + 1) * BLOCK)
        sp = [split(x) for x in (s0[...], s1[...], s2[...])]
        gp = [split(x) for x in (g[0], g[1], g21[...])]
        sub_cols = 2 * LANES
        totals = [jnp.zeros((SUB, sub_cols), F32) for _ in range(PICKS)]
        for t in range(cols // sub_cols):
            cs = slice(t * sub_cols, (t + 1) * sub_cols)
            w0h, w0l = wh[e(0), cs], wl[e(0), cs]
            v0 = ws[e(0), cs]
            v1 = ws[e(1), cs] - dot3(*gp[0], w0h, w0l)
            v1h, v1l = split(v1)
            v2 = ws[e(2), cs] - dot3(*gp[1], w0h, w0l) - dot3(*gp[2], v1h, v1l)
            for i, (v, vh, vl) in enumerate(((v0, w0h, w0l), (v1, v1h, v1l), (v2, *split(v2)))):
                prod = v * dot3(*sp[i], vh, vl)
                totals[i] = totals[i] + jnp.sum(prod.reshape(BLOCK // SUB, SUB, sub_cols), axis=0)
        scale = 1.0 / (2.0 * BLOCK * cols)
        for i in range(PICKS):
            loss[i] = jnp.sum(totals[i]) * scale

    rows = first + pl.program_id(0) * tile + lax.broadcasted_iota(jnp.int32, (tile, LANES), 0)
    block_of = rows // BLOCK
    listed = (block_of == 0) | (block_of == sc[6]) | (block_of == sc[7])
    keep = jnp.where(listed, 0.0, 1.0)[:, :1] > 0.5
    res = w_ref[...] - dot3(th[...], tl[...], wh[...], wl[...])
    o_ref[...] = jnp.where(keep, res, 0.0)


VMEM = pl.BlockSpec(memory_space=pltpu.VMEM)
SMEM = pl.BlockSpec(memory_space=pltpu.SMEM)
ANY = pl.BlockSpec(memory_space=pl.ANY)
BIG = pltpu.CompilerParams(vmem_limit_bytes=56 << 20)


def shape(*dims, dtype=F32):
    return jax.ShapeDtypeStruct(dims, dtype)


def square(n):
    return shape(n, BLOCK, BLOCK)


def run_first(sc, mine, other):
    return pl.pallas_call(
        first_kernel,
        out_shape=(shape(BLOCK, BLOCK), square(2), square(3)),
        in_specs=[SMEM, VMEM, VMEM],
        out_specs=(VMEM, VMEM, VMEM),
        scratch_shapes=[
            pltpu.VMEM((2, BLOCK, PICKS * BLOCK), F32),
            pltpu.VMEM((2, BLOCK, HALF), F32),
            pltpu.VMEM((PICKS, PICKS, BLOCK, BLOCK), F32),
        ],
        compiler_params=BIG,
        name="first_pick",
    )(sc, mine, other)


def run_second(a):
    one = shape(BLOCK, BLOCK)
    return pl.pallas_call(
        second_kernel, out_shape=(one, one, one), in_specs=[VMEM], out_specs=(VMEM,) * 3, compiler_params=BIG, name="second_pick"
    )(a)


def run_third(*args):
    n = PICKS * BLOCK
    return pl.pallas_call(
        third_kernel, out_shape=(shape(BLOCK, BLOCK), shape(n, n)), in_specs=[VMEM] * 5, out_specs=(VMEM,) * 2, compiler_params=BIG, name="third_pick"
    )(*args)


def tile_of(rows):
    return max(t for t in range(SUB, 257, SUB) if rows % t == 0)


def run_left(k, panels):
    rows, n = panels.shape
    tile = tile_of(rows)
    spec = pl.BlockSpec((tile, n), lambda i: (i, 0))
    return pl.pallas_call(
        left_kernel,
        grid=(rows // tile,),
        out_shape=(shape(rows, n, dtype=BF16),) * 2,
        in_specs=[VMEM, spec],
        out_specs=(spec, spec),
        scratch_shapes=[pltpu.VMEM((n, n), BF16)] * 2,
        compiler_params=BIG,
        name="left_factor",
    )(k, panels)


def run_final(sc, weights, th, tl, fl_mine, fl_other, m_mine, m_other, s0, s1, s2, g, g21):
    rows, cols = weights.shape
    n = PICKS * BLOCK
    tile = tile_of(rows)
    n_chip = fl_mine.shape[0]
    wide = pl.BlockSpec((tile, cols), lambda i: (i, 0))
    left = pl.BlockSpec((tile, n), lambda i: (i, 0))
    return pl.pallas_call(
        final_kernel,
        grid=(rows // tile,),
        out_shape=(shape(rows, cols), shape(PICKS)),
        in_specs=[SMEM, wide, left, left, ANY, ANY, ANY, ANY] + [VMEM] * 5,
        out_specs=(wide, SMEM),
        scratch_shapes=[
            pltpu.VMEM((n, cols), F32),
            pltpu.VMEM((n, cols), BF16),
            pltpu.VMEM((n, cols), BF16),
            pltpu.SemaphoreType.DMA((n_chip, 4)),
        ],
        compiler_params=BIG,
        name="final_update",
    )(sc, weights, th, tl, fl_mine, fl_other, m_mine, m_other, s0, s1, s2, g, g21)


def body(n_row, panels, weights, block_ids):
    local, cols = weights.shape
    n_chip = n_row // 2
    s = BLOCK // n_chip
    idx = lax.axis_index("row")
    core, chip = idx % 2, idx // 2
    last = n_row - 1
    first_row = idx * local
    last_block = n_row * local // BLOCK - 1

    c_f = jnp.argmax(block_ids == 0).astype(jnp.int32)
    c_l = jnp.argmax(block_ids == last_block).astype(jnp.int32)
    c_m = PICKS - c_f - c_l
    mid_block = jnp.sum(block_ids) - last_block
    sc = jnp.stack([core, chip, c_f, c_l, c_m, first_row, jnp.int32(last_block), mid_block]).astype(jnp.int32)

    def swap(x, bit):
        return lax.ppermute(x, "row", [(i, i ^ bit) for i in range(n_row)])

    is_last = idx == last

    def scatter(array):
        base = jnp.where(is_last, local - BLOCK, 0)
        own_slice = jnp.where(is_last, n_chip - 1, 0)
        out = lax.dynamic_slice_in_dim(array, base + own_slice * s, s, 0)
        out = jnp.where((idx == 0) | is_last, out, 0.0)
        for k in range(1, n_chip):
            piece = lax.dynamic_slice_in_dim(array, base + jnp.where(is_last, n_chip - 1 - k, k) * s, s, 0)
            out = out + lax.ppermute(piece, "row", [(0, 2 * k), (last, last - 2 * k)])
        return out

    start = mid_block * BLOCK - first_row
    clipped = jnp.clip(start, 0, local - BLOCK)
    shift = start - clipped

    def masked(array, col, width):
        got = lax.dynamic_slice(array, (clipped, col), (BLOCK, width))
        got = jnp.pad(got, ((BLOCK, BLOCK), (0, 0)))
        return lax.dynamic_slice_in_dim(got, BLOCK + jnp.clip(shift, -BLOCK, BLOCK), BLOCK, 0)

    def halve(x):
        width = x.shape[1] // 2
        keep = lax.dynamic_slice_in_dim(x, core * width, width, 1)
        send = lax.dynamic_slice_in_dim(x, (1 - core) * width, width, 1)
        x = keep + swap(send, 1)
        bit = 1
        x = x.reshape(n_chip, s, width)
        done = 0
        while bit < n_chip:
            half = x.reshape(x.shape[0] // 2, 2, s, width)
            mine = (chip // bit) % 2
            keep = lax.dynamic_index_in_dim(half, mine, 1, keepdims=False)
            send = lax.dynamic_index_in_dim(half, 1 - mine, 1, keepdims=False)
            x = keep + swap(send, 2 * bit)
            bit *= 2
        return x.reshape(s, width)

    a_line = scatter(panels)
    a_mid = halve(masked(panels, c_m * BLOCK, BLOCK))
    a_own = jnp.concatenate([a_line, a_mid], axis=1)

    a_parts = [a_own] + [swap(a_own, 2 * k) for k in range(1, n_chip)]
    a_mine = jnp.stack(a_parts)
    a_other = swap(a_mine, 1)

    w_line = scatter(weights)
    w_mid = halve(masked(weights, 0, cols))
    w_line, w_mid, a_other = lax.optimization_barrier((w_line, w_mid, a_other))

    def z_gather(parts):
        out = []
        for k in range(n_chip // 2):
            out.append([p if k == 0 else swap(p, 4 * k) for p in parts])
        return out

    m_y = swap(w_mid, 2)
    m_parts = jnp.stack([w_mid, m_y])
    m_z = [m_parts] + [swap(m_parts, 4 * k) for k in range(1, n_chip // 2)]
    m_mine = jnp.concatenate(m_z, axis=0)
    f_z = jnp.stack([w_line] + [swap(w_line, 4 * k) for k in range(1, n_chip // 2)])
    f_y = swap(f_z, 2)
    fl_mine = jnp.stack([f_z, f_y], axis=1).reshape(n_chip, s, cols)
    m_other = swap(m_mine, 1)
    fl_other = swap(fl_mine, 1)

    s0, g, a1 = run_first(sc, a_mine, a_other)
    s1, g21, a2 = run_second(a1)
    s2, k = run_third(a2, s0, s1, g, g21)
    th, tl = run_left(k, panels)
    return run_final(sc, weights, th, tl, fl_mine, fl_other, m_mine, m_other, s0, s1, s2, g, g21)


def solution(mesh):
    n_row = mesh.shape["row"]
    rows = P(("groups", "row"), None)
    return jax.shard_map(
        functools.partial(body, n_row),
        mesh=mesh,
        in_specs=(rows, rows, P("groups")),
        out_specs=(rows, P("groups")),
        check_vma=False,
    )
```

```python
import functools

import jax
import jax.numpy as jnp
from jax import lax
from jax.experimental import pallas as pl
from jax.experimental.pallas import tpu as pltpu
from jax.sharding import PartitionSpec as P

BLOCK = 256
PICKS = 3
HALF = BLOCK // 2
SUB = 8
LANES = 128
EXACT = lax.Precision.HIGHEST
F32 = jnp.float32
BF16 = jnp.bfloat16


def mm(a, b):
    return lax.dot_general(a, b, (((1,), (0,)), ((), ())), precision=EXACT, preferred_element_type=F32)


def mm_nt(a, b):
    return lax.dot_general(a, b, (((1,), (1,)), ((), ())), precision=EXACT, preferred_element_type=F32)


def mm_tn(a, b):
    return lax.dot_general(a, b, (((0,), (0,)), ((), ())), precision=EXACT, preferred_element_type=F32)


def lane_bcast(x, c):
    return jnp.broadcast_to(x[:, c : c + 1], (SUB, LANES))


def row_bcast(x, j):
    return jnp.broadcast_to(x[j : j + 1, :], (SUB, LANES))


def inv_half(m):
    n_panels = HALF // SUB
    rows = [m[SUB * i : SUB * i + SUB, :] for i in range(n_panels)]
    lane = lax.broadcasted_iota(jnp.int32, (SUB, LANES), 1)
    sub = lax.broadcasted_iota(jnp.int32, (SUB, LANES), 0)
    for p in range(n_panels):
        panel = rows[p]
        cols = [lane_bcast(panel, SUB * p + k) for k in range(SUB)]
        for j in range(SUB):
            is_j = sub == j
            r = 1.0 / row_bcast(cols[j], j)
            f = cols[j] * r
            panel = jnp.where(lane == SUB * p + j, jnp.where(is_j, 1.0, 0.0), panel)
            u = row_bcast(panel, j)
            panel = jnp.where(is_j, u * r, panel - f * u)
            for k in range(j + 1, SUB):
                uk = row_bcast(cols[k], j)
                cols[k] = jnp.where(is_j, uk * r, cols[k] - f * uk)
        reps = [row_bcast(panel, k) for k in range(SUB)]
        in_panel = (lane >= SUB * p) & (lane < SUB * p + SUB)
        for step in range(1, n_panels):
            i = (p + step) % n_panels
            t = [lane_bcast(rows[i], SUB * p + k) * reps[k] for k in range(SUB)]
            total = ((t[0] + t[1]) + (t[2] + t[3])) + ((t[4] + t[5]) + (t[6] + t[7]))
            rows[i] = jnp.where(in_panel, 0.0, rows[i]) - total
        rows[p] = panel
    return jnp.concatenate(rows, axis=0)


def inv_block(ref, half_in, half_out):
    def one(h, _):
        @pl.when(h == 0)
        def _():
            half_in[...] = ref[:HALF, :HALF]

        @pl.when(h == 1)
        def _():
            c = ref[HALF:, :HALF]
            half_in[...] = ref[HALF:, HALF:] - mm_nt(mm(c, half_out[0]), c)

        half_out[h] = inv_half(half_in[...])
        return 0

    lax.fori_loop(0, 2, one, 0)
    ai, si = half_out[0], half_out[1]
    g = mm(ref[HALF:, :HALF], ai)
    h = mm(si, g)
    top = jnp.concatenate([ai + mm_tn(g, h), -h.T], axis=1)
    return jnp.concatenate([top, jnp.concatenate([-h, si], axis=1)], axis=0)


def split(x):
    hi = x.astype(BF16)
    return hi, (x - hi.astype(F32)).astype(BF16)


def dot3k(stacked_left, stacked_right):
    return jnp.dot(stacked_left, stacked_right, preferred_element_type=F32)


def left3(x):
    hi, lo = split(x)
    return jnp.concatenate([hi, hi, lo], axis=1)


def right3(x):
    hi, lo = split(x)
    return jnp.concatenate([hi, lo, hi], axis=0)


def positions(n_row, local, ids):
    last_block = n_row * local // BLOCK - 1
    at = lambda v: jnp.where(ids[0] == v, 0, jnp.where(ids[1] == v, 1, 2)).astype(jnp.int32)
    c_f, c_l = at(0), at(last_block)
    return c_f, c_l, PICKS - c_f - c_l, ids[0] + ids[1] + ids[2] - last_block


def pack_kernel(n_row, picked, ids, src, line_out, keep_out, send_out, zero, sems):
    local, cols = src.shape
    idx = lax.axis_index("row")
    core = idx % 2
    _, _, c_m, mid = positions(n_row, local, ids)
    grain = min(BLOCK, local & -local)
    width = keep_out.shape[1]
    base = jnp.where(idx == n_row - 1, local - BLOCK, 0)
    line = pltpu.make_async_copy(src.at[pl.ds(pl.multiple_of(base, SUB), BLOCK), :], line_out, sems.at[0])
    line.start()
    zero[...] = jnp.zeros_like(zero)
    left = c_m * BLOCK if picked else 0
    for i in range(BLOCK // grain):
        row = mid * BLOCK + i * grain - idx * local
        owned = (row >= 0) & (row < local)
        for j, (out, side) in enumerate(((keep_out, core), (send_out, 1 - core))):
            dst = out.at[pl.ds(i * grain, grain), :]
            sem = sems.at[1 + 2 * i + j]

            @pl.when(owned)
            def _():
                at = src.at[pl.ds(pl.multiple_of(row, SUB), grain), pl.ds(pl.multiple_of(left + side * width, LANES), width)]
                pltpu.make_async_copy(at, dst, sem).start()

            @pl.when(jnp.logical_not(owned))
            def _():
                pltpu.make_async_copy(zero, dst, sem).start()

    for i in range(BLOCK // grain):
        for j, out in enumerate((keep_out, send_out)):
            pltpu.make_async_copy(zero, out.at[pl.ds(i * grain, grain), :], sems.at[1 + 2 * i + j]).wait()
    line.wait()


def first_kernel(n_row, local, ids, mine, other, s_out, g_out, a_out, fl, mid, blk, half_in, half_out):
    idx = lax.axis_index("row")
    core, chip = idx % 2, idx // 2
    c_f, c_l, c_m, _ = positions(n_row, local, ids)
    n_chip, s = mine.shape[0], mine.shape[1]
    width = PICKS * BLOCK
    for k in range(n_chip):
        row = pl.multiple_of((chip ^ k) * s, SUB)
        fl[core, pl.ds(row, s), :] = mine[k, :, :width]
        mid[core, pl.ds(row, s), :] = mine[k, :, width:]
        fl[1 - core, pl.ds(row, s), :] = other[k, :, :width]
        mid[1 - core, pl.ds(row, s), :] = other[k, :, width:]
    for j in range(PICKS):
        blk[c_f, j] = fl[0, :, j * BLOCK : (j + 1) * BLOCK]
        blk[c_l, j] = fl[1, :, j * BLOCK : (j + 1) * BLOCK]
    blk[c_m, c_f] = blk[c_f, c_m].T
    blk[c_m, c_l] = blk[c_l, c_m].T
    blk[c_m, c_m, :, :HALF] = mid[0]
    blk[c_m, c_m, :, HALF:] = mid[1]
    s0 = inv_block(blk.at[0, 0], half_in, half_out)
    s_out[...] = s0
    a10, a20 = blk[1, 0], blk[2, 0]
    g10, g20 = mm(a10, s0), mm(a20, s0)
    g_out[0] = g10
    g_out[1] = g20
    a_out[0] = blk[1, 1] - mm_nt(g10, a10)
    a_out[1] = blk[2, 1] - mm_nt(g20, a10)
    a_out[2] = blk[2, 2] - mm_nt(g20, a20)


def second_kernel(a_in, s_out, g_out, a_out, half_in, half_out):
    s1 = inv_block(a_in.at[0], half_in, half_out)
    s_out[...] = s1
    a21 = a_in[1]
    g21 = mm(a21, s1)
    g_out[...] = g21
    a_out[...] = a_in[2] - mm_nt(g21, a21)


def third_kernel(a_in, s0, s1, g, g21, s_out, k_out, half_in, half_out):
    s2 = inv_block(a_in, half_in, half_out)
    s_out[...] = s2
    g10, g20 = g[0], g[1]
    j21 = -g21[...]
    j20 = mm(g21[...], g10) - g20
    k21, k20 = mm(s2, j21), mm(s2, j20)
    t10 = mm(s1[...], g10)
    k11 = s1[...] + mm_tn(j21, k21)
    k10 = mm_tn(j21, k20) - t10
    k00 = s0[...] + mm_tn(g10, t10) + mm_tn(j20, k20)
    e = lambda i: slice(i * BLOCK, (i + 1) * BLOCK)
    k_out[e(2), e(2)] = s2
    k_out[e(2), e(1)] = k21
    k_out[e(1), e(2)] = k21.T
    k_out[e(2), e(0)] = k20
    k_out[e(0), e(2)] = k20.T
    k_out[e(1), e(1)] = k11
    k_out[e(1), e(0)] = k10
    k_out[e(0), e(1)] = k10.T
    k_out[e(0), e(0)] = k00


def left_kernel(k_ref, p_ref, hi_out, lo_out, k3):
    @pl.when(pl.program_id(0) == 0)
    def _():
        k3[...] = right3(k_ref[...])

    hi_out[...], lo_out[...] = split(dot3k(left3(p_ref[...]), k3[...]))


def final_kernel(n_row, ids, w_ref, th, tl, fl_mine, fl_other, m_mine, m_other, s0, s1, s2, g, g21, o_ref, loss, ws, w3, sems):
    tile, cols = o_ref.shape
    local = pl.num_programs(0) * tile
    n_chip, s = fl_mine.shape[0], fl_mine.shape[1]
    idx = lax.axis_index("row")
    core, chip = idx % 2, idx // 2
    c_f, c_l, c_m, mid_block = positions(n_row, local, ids)
    n = PICKS * BLOCK

    @pl.when(pl.program_id(0) == 0)
    def _():
        copies = []
        half_cols = cols // 2
        mine_at = jnp.where(core == 0, c_f, c_l) * BLOCK
        other_at = jnp.where(core == 0, c_l, c_f) * BLOCK
        mine_col = pl.multiple_of(core * half_cols, LANES)
        other_col = pl.multiple_of((1 - core) * half_cols, LANES)
        for k in range(n_chip):
            row = (chip ^ k) * s
            at = lambda base: pl.ds(pl.multiple_of(base + row, SUB), s)
            copies.append(pltpu.make_async_copy(fl_mine.at[k], ws.at[at(mine_at), :], sems.at[k, 0]))
            copies.append(pltpu.make_async_copy(fl_other.at[k], ws.at[at(other_at), :], sems.at[k, 1]))
            copies.append(pltpu.make_async_copy(m_mine.at[k], ws.at[at(c_m * BLOCK), pl.ds(mine_col, half_cols)], sems.at[k, 2]))
            copies.append(pltpu.make_async_copy(m_other.at[k], ws.at[at(c_m * BLOCK), pl.ds(other_col, half_cols)], sems.at[k, 3]))
        for c in copies:
            c.start()
        for c in copies:
            c.wait()
        hi, lo = split(ws[...])
        w3[:n] = hi
        w3[n : 2 * n] = lo
        w3[2 * n :] = hi
        e = lambda i: slice(i * BLOCK, (i + 1) * BLOCK)
        sp = [left3(x) for x in (s0[...], s1[...], s2[...])]
        gp = [left3(x) for x in (g[0], g[1], g21[...])]
        sub_cols = 2 * LANES
        totals = [jnp.zeros((SUB, sub_cols), F32) for _ in range(PICKS)]
        for t in range(cols // sub_cols):
            cs = slice(t * sub_cols, (t + 1) * sub_cols)
            v0 = ws[e(0), cs]
            r0 = right3(v0)
            v1 = ws[e(1), cs] - dot3k(gp[0], r0)
            r1 = right3(v1)
            v2 = ws[e(2), cs] - dot3k(gp[1], r0) - dot3k(gp[2], r1)
            for i, (v, r) in enumerate(((v0, r0), (v1, r1), (v2, right3(v2)))):
                prod = v * dot3k(sp[i], r)
                totals[i] = totals[i] + jnp.sum(prod.reshape(BLOCK // SUB, SUB, sub_cols), axis=0)
        scale = 1.0 / (2.0 * BLOCK * cols)
        for i in range(PICKS):
            loss[i] = jnp.sum(totals[i]) * scale

    first = idx * local + pl.program_id(0) * tile
    block_of = (first + lax.broadcasted_iota(jnp.int32, (tile, 1), 0)) // BLOCK
    listed = (block_of == 0) | (block_of == n_row * local // BLOCK - 1) | (block_of == mid_block)
    t3 = jnp.concatenate([th[...], th[...], tl[...]], axis=1)
    res = w_ref[...] - dot3k(t3, w3[...])
    o_ref[...] = jnp.where(listed, 0.0, res)


VMEM = pl.BlockSpec(memory_space=pltpu.VMEM)
SMEM = pl.BlockSpec(memory_space=pltpu.SMEM)
ANY = pl.BlockSpec(memory_space=pl.ANY)
BIG = pltpu.CompilerParams(vmem_limit_bytes=56 << 20)


def shape(*dims, dtype=F32):
    return jax.ShapeDtypeStruct(dims, dtype)


def square(n):
    return shape(n, BLOCK, BLOCK)


HALVES = [pltpu.VMEM((HALF, HALF), F32), pltpu.VMEM((2, HALF, HALF), F32)]


def cost(us):
    return pl.CostEstimate(flops=int(us * 1e9), bytes_accessed=1 << 20, transcendentals=0)


def run_pack(n_row, picked, ids, src):
    local, cols = src.shape
    width = (BLOCK if picked else cols) // 2
    grain = min(BLOCK, local & -local)
    half = shape(BLOCK, width)
    return pl.pallas_call(
        functools.partial(pack_kernel, n_row, picked),
        out_shape=(shape(BLOCK, cols), half, half),
        in_specs=[SMEM, ANY],
        out_specs=(ANY, ANY, ANY),
        scratch_shapes=[pltpu.VMEM((grain, width), F32), pltpu.SemaphoreType.DMA((1 + 2 * (BLOCK // grain),))],
        compiler_params=BIG,
        name="pack_panels" if picked else "pack_weights",
    )(ids, src)


def run_first(n_row, local, ids, mine, other):
    return pl.pallas_call(
        functools.partial(first_kernel, n_row, local),
        out_shape=(shape(BLOCK, BLOCK), square(2), square(3)),
        in_specs=[SMEM, VMEM, VMEM],
        out_specs=(VMEM, VMEM, VMEM),
        scratch_shapes=[
            pltpu.VMEM((2, BLOCK, PICKS * BLOCK), F32),
            pltpu.VMEM((2, BLOCK, HALF), F32),
            pltpu.VMEM((PICKS, PICKS, BLOCK, BLOCK), F32),
        ]
        + HALVES,
        compiler_params=BIG,
        cost_estimate=cost(13),
        name="first_pick",
    )(ids, mine, other)


def run_second(a):
    one = shape(BLOCK, BLOCK)
    return pl.pallas_call(
        second_kernel,
        out_shape=(one, one, one),
        in_specs=[VMEM],
        out_specs=(VMEM,) * 3,
        scratch_shapes=HALVES,
        compiler_params=BIG,
        cost_estimate=cost(12),
        name="second_pick",
    )(a)


def run_third(*args):
    n = PICKS * BLOCK
    return pl.pallas_call(
        third_kernel,
        out_shape=(shape(BLOCK, BLOCK), shape(n, n)),
        in_specs=[VMEM] * 5,
        out_specs=(VMEM,) * 2,
        scratch_shapes=HALVES,
        compiler_params=BIG,
        cost_estimate=cost(14),
        name="third_pick",
    )(*args)


def tile_of(rows):
    return max(t for t in range(SUB, 2 * BLOCK + 1, SUB) if rows % t == 0)


def run_left(k, panels):
    rows, n = panels.shape
    tile = tile_of(rows)
    spec = pl.BlockSpec((tile, n), lambda i: (i, 0))
    return pl.pallas_call(
        left_kernel,
        grid=(rows // tile,),
        out_shape=(shape(rows, n, dtype=BF16),) * 2,
        in_specs=[VMEM, spec],
        out_specs=(spec, spec),
        scratch_shapes=[pltpu.VMEM((3 * n, n), BF16)],
        compiler_params=BIG,
        cost_estimate=cost(10),
        name="left_factor",
    )(k, panels)


def run_final(n_row, ids, weights, th, tl, fl_mine, fl_other, m_mine, m_other, s0, s1, s2, g, g21):
    rows, cols = weights.shape
    n = PICKS * BLOCK
    tile = tile_of(rows)
    n_chip = fl_mine.shape[0]
    wide = pl.BlockSpec((tile, cols), lambda i: (i, 0))
    left = pl.BlockSpec((tile, n), lambda i: (i, 0))
    return pl.pallas_call(
        functools.partial(final_kernel, n_row),
        grid=(rows // tile,),
        out_shape=(shape(rows, cols), shape(PICKS)),
        in_specs=[SMEM, wide, left, left, ANY, ANY, ANY, ANY] + [VMEM] * 5,
        out_specs=(wide, SMEM),
        scratch_shapes=[
            pltpu.VMEM((n, cols), F32),
            pltpu.VMEM((3 * n, cols), BF16),
            pltpu.SemaphoreType.DMA((n_chip, 4)),
        ],
        compiler_params=BIG,
        cost_estimate=cost(20),
        name="final_update",
    )(ids, weights, th, tl, fl_mine, fl_other, m_mine, m_other, s0, s1, s2, g, g21)


def body(n_row, panels, weights, block_ids):
    local, cols = weights.shape
    n_chip = n_row // 2
    s = BLOCK // n_chip
    idx = lax.axis_index("row")
    core, chip = idx & 1, idx >> 1
    last = n_row - 1

    def swap(x, bit):
        return lax.ppermute(x, "row", [(i, i ^ bit) for i in range(n_row)])

    def parts(x, bit_value):
        half = x.shape[0] // 2
        keep = lax.dynamic_slice_in_dim(x, bit_value * half, half, 0)
        return keep, lax.dynamic_slice_in_dim(x, (1 - bit_value) * half, half, 0)

    from_root = jnp.where(core == 0, chip, n_chip - 1 - chip)

    def scatter(x):
        bit = n_chip // 2
        while bit:
            keep, send = parts(x, (chip // bit) & 1)
            pairs = []
            for c in range(0, n_chip, 2 * bit):
                pairs += [(2 * c, 2 * (c + bit)), (last - 2 * c, last - 2 * (c + bit))]
            got = lax.ppermute(send, "row", pairs)
            x = jnp.where(from_root % (2 * bit) == bit, got, keep)
            bit //= 2
        return x

    def halve(keep, send):
        x = (keep + swap(send, 1)).reshape(n_chip, s, keep.shape[1])
        bit = 1
        while bit < n_chip:
            half = x.reshape(x.shape[0] // 2, 2, s, x.shape[2])
            mine = (chip // bit) & 1
            keep = lax.dynamic_index_in_dim(half, mine, 1, keepdims=False)
            send = lax.dynamic_index_in_dim(half, 1 - mine, 1, keepdims=False)
            x = keep + swap(send, 2 * bit)
            bit *= 2
        return x.reshape(s, x.shape[2])

    with jax.named_scope("a_move"):
        a_block, a_keep, a_send = run_pack(n_row, True, block_ids, panels)
        a_own = jnp.concatenate([scatter(a_block), halve(a_keep, a_send)], axis=1)
        a_mine = jnp.stack([a_own] + [swap(a_own, 2 * k) for k in range(1, n_chip)])
        a_other = swap(a_mine, 1)

    with jax.named_scope("w_spread"):
        w_block, w_keep, w_send = run_pack(n_row, False, block_ids, weights)
        w_line = scatter(w_block)
        w_mid = halve(w_keep, w_send)

    n_z = n_chip // 2
    with jax.named_scope("w_gather"):
        w_line, a_mine, a_other = lax.optimization_barrier((w_line, a_mine, a_other))
        m_parts = jnp.stack([w_mid, swap(w_mid, 2)])
        m_mine = jnp.concatenate([m_parts] + [swap(m_parts, 4 * k) for k in range(1, n_z)], axis=0)
        f_z = jnp.stack([w_line] + [swap(w_line, 4 * k) for k in range(1, n_z)])
        fl_mine = jnp.stack([f_z, swap(f_z, 2)], axis=1).reshape(n_chip, s, cols)
        m_other = swap(m_mine, 1)
        fl_other = swap(fl_mine, 1)

    s0, g, a1 = run_first(n_row, local, block_ids, a_mine, a_other)
    s1, g21, a2 = run_second(a1)
    s2, k = run_third(a2, s0, s1, g, g21)
    th, tl = run_left(k, panels)
    return run_final(n_row, block_ids, weights, th, tl, fl_mine, fl_other, m_mine, m_other, s0, s1, s2, g, g21)


def solution(mesh):
    n_row = mesh.shape["row"]
    rows = P(("groups", "row"), None)
    return jax.shard_map(
        functools.partial(body, n_row),
        mesh=mesh,
        in_specs=(rows, rows, P("groups")),
        out_specs=(rows, P("groups")),
        check_vma=False,
    )
```

```python
import functools

import jax
import jax.numpy as jnp
from jax import lax
from jax.experimental import pallas as pl
from jax.experimental.pallas import tpu as pltpu
from jax.sharding import PartitionSpec as P

BLOCK = 256
PICKS = 3
HALF = BLOCK // 2
SUB = 8
LANES = 128
EXACT = lax.Precision.HIGHEST
F32 = jnp.float32
BF16 = jnp.bfloat16


def mm(a, b):
    return lax.dot_general(a, b, (((1,), (0,)), ((), ())), precision=EXACT, preferred_element_type=F32)


def mm_nt(a, b):
    return lax.dot_general(a, b, (((1,), (1,)), ((), ())), precision=EXACT, preferred_element_type=F32)


def mm_tn(a, b):
    return lax.dot_general(a, b, (((0,), (0,)), ((), ())), precision=EXACT, preferred_element_type=F32)


def lane_bcast(x, c):
    return jnp.broadcast_to(x[:, c : c + 1], (SUB, LANES))


def row_bcast(x, j):
    return jnp.broadcast_to(x[j : j + 1, :], (SUB, LANES))


def inv_half(m):
    n_panels = HALF // SUB
    rows = [m[SUB * i : SUB * i + SUB, :] for i in range(n_panels)]
    lane = lax.broadcasted_iota(jnp.int32, (SUB, LANES), 1)
    sub = lax.broadcasted_iota(jnp.int32, (SUB, LANES), 0)
    for p in range(n_panels):
        panel = rows[p]
        cols = [lane_bcast(panel, SUB * p + k) for k in range(SUB)]
        for j in range(SUB):
            is_j = sub == j
            r = 1.0 / row_bcast(cols[j], j)
            f = cols[j] * r
            panel = jnp.where(lane == SUB * p + j, jnp.where(is_j, 1.0, 0.0), panel)
            u = row_bcast(panel, j)
            panel = jnp.where(is_j, u * r, panel - f * u)
            for k in range(j + 1, SUB):
                uk = row_bcast(cols[k], j)
                cols[k] = jnp.where(is_j, uk * r, cols[k] - f * uk)
        reps = [row_bcast(panel, k) for k in range(SUB)]
        in_panel = (lane >= SUB * p) & (lane < SUB * p + SUB)
        for step in range(1, n_panels):
            i = (p + step) % n_panels
            t = [lane_bcast(rows[i], SUB * p + k) * reps[k] for k in range(SUB)]
            total = ((t[0] + t[1]) + (t[2] + t[3])) + ((t[4] + t[5]) + (t[6] + t[7]))
            rows[i] = jnp.where(in_panel, 0.0, rows[i]) - total
        rows[p] = panel
    return jnp.concatenate(rows, axis=0)


def inv_block(ref, half_in, half_out):
    def one(h, _):
        @pl.when(h == 0)
        def _():
            half_in[...] = ref[:HALF, :HALF]

        @pl.when(h == 1)
        def _():
            c = ref[HALF:, :HALF]
            half_in[...] = ref[HALF:, HALF:] - mm_nt(mm(c, half_out[0]), c)

        half_out[h] = inv_half(half_in[...])
        return 0

    lax.fori_loop(0, 2, one, 0)
    ai, si = half_out[0], half_out[1]
    g = mm(ref[HALF:, :HALF], ai)
    h = mm(si, g)
    top = jnp.concatenate([ai + mm_tn(g, h), -h.T], axis=1)
    return jnp.concatenate([top, jnp.concatenate([-h, si], axis=1)], axis=0)


def split(x):
    hi = x.astype(BF16)
    return hi, (x - hi.astype(F32)).astype(BF16)


def dot3k(stacked_left, stacked_right):
    return jnp.dot(stacked_left, stacked_right, preferred_element_type=F32)


def left3(x):
    hi, lo = split(x)
    return jnp.concatenate([hi, hi, lo], axis=1)


def right3(x):
    hi, lo = split(x)
    return jnp.concatenate([hi, lo, hi], axis=0)


def positions(n_row, local, ids):
    last_block = n_row * local // BLOCK - 1
    at = lambda v: jnp.where(ids[0] == v, 0, jnp.where(ids[1] == v, 1, 2)).astype(jnp.int32)
    c_f, c_l = at(0), at(last_block)
    return c_f, c_l, PICKS - c_f - c_l, ids[0] + ids[1] + ids[2] - last_block


def pack_kernel(n_row, picked, ids, src, line_out, keep_out, send_out, sems):
    local, cols = src.shape
    idx = lax.axis_index("row")
    core = idx & 1
    _, _, c_m, mid = positions(n_row, local, ids)
    grain = min(BLOCK, local & -local)
    width = keep_out.shape[1]
    base = jnp.where(idx == n_row - 1, local - BLOCK, 0)
    line = pltpu.make_async_copy(src.at[pl.ds(pl.multiple_of(base, SUB), BLOCK), :], line_out, sems.at[0])
    line.start()
    left = c_m * BLOCK if picked else 0

    def copy(i, out, side, sem):
        row = pl.multiple_of(mid * BLOCK + i * grain - idx * local, SUB)
        at = src.at[pl.ds(row, grain), pl.ds(pl.multiple_of(left + side * width, LANES), width)]
        return pltpu.make_async_copy(at, out.at[pl.ds(i * grain, grain), :], sem)

    def each(act):
        for i in range(BLOCK // grain):
            row = mid * BLOCK + i * grain - idx * local
            owned = (row >= 0) & (row < local)
            for j, (out, side) in enumerate(((keep_out, core), (send_out, 1 - core))):
                act(i, out, side, sems.at[1 + 2 * i + j], owned)

    def begin(i, out, side, sem, owned):
        @pl.when(owned)
        def _():
            copy(i, out, side, sem).start()

        @pl.when(jnp.logical_not(owned))
        def _():
            out[i * grain : (i + 1) * grain, :] = jnp.zeros((grain, width), F32)

    def finish(i, out, side, sem, owned):
        @pl.when(owned)
        def _():
            copy(i, out, side, sem).wait()

    each(begin)
    each(finish)
    line.wait()


def first_kernel(n_row, local, ids, mine, other, s_out, g_out, a_out, fl, mid, blk, half_in, half_out):
    idx = lax.axis_index("row")
    core, chip = idx % 2, idx // 2
    c_f, c_l, c_m, _ = positions(n_row, local, ids)
    n_chip, s = mine.shape[0], mine.shape[1]
    width = PICKS * BLOCK
    for k in range(n_chip):
        row = pl.multiple_of((chip ^ k) * s, SUB)
        fl[core, pl.ds(row, s), :] = mine[k, :, :width]
        mid[core, pl.ds(row, s), :] = mine[k, :, width:]
        fl[1 - core, pl.ds(row, s), :] = other[k, :, :width]
        mid[1 - core, pl.ds(row, s), :] = other[k, :, width:]
    for j in range(PICKS):
        blk[c_f, j] = fl[0, :, j * BLOCK : (j + 1) * BLOCK]
        blk[c_l, j] = fl[1, :, j * BLOCK : (j + 1) * BLOCK]
    blk[c_m, c_f] = blk[c_f, c_m].T
    blk[c_m, c_l] = blk[c_l, c_m].T
    blk[c_m, c_m, :, :HALF] = mid[0]
    blk[c_m, c_m, :, HALF:] = mid[1]
    s0 = inv_block(blk.at[0, 0], half_in, half_out)
    s_out[...] = s0
    a10, a20 = blk[1, 0], blk[2, 0]
    g10, g20 = mm(a10, s0), mm(a20, s0)
    g_out[0] = g10
    g_out[1] = g20
    a_out[0] = blk[1, 1] - mm_nt(g10, a10)
    a_out[1] = blk[2, 1] - mm_nt(g20, a10)
    a_out[2] = blk[2, 2] - mm_nt(g20, a20)


def second_kernel(a_in, s_out, g_out, a_out, half_in, half_out):
    s1 = inv_block(a_in.at[0], half_in, half_out)
    s_out[...] = s1
    a21 = a_in[1]
    g21 = mm(a21, s1)
    g_out[...] = g21
    a_out[...] = a_in[2] - mm_nt(g21, a21)


def third_kernel(a_in, s0, s1, g, g21, s_out, k_out, half_in, half_out):
    s2 = inv_block(a_in, half_in, half_out)
    s_out[...] = s2
    g10, g20 = g[0], g[1]
    j21 = -g21[...]
    j20 = mm(g21[...], g10) - g20
    k21, k20 = mm(s2, j21), mm(s2, j20)
    t10 = mm(s1[...], g10)
    k11 = s1[...] + mm_tn(j21, k21)
    k10 = mm_tn(j21, k20) - t10
    k00 = s0[...] + mm_tn(g10, t10) + mm_tn(j20, k20)
    e = lambda i: slice(i * BLOCK, (i + 1) * BLOCK)
    k_out[e(2), e(2)] = s2
    k_out[e(2), e(1)] = k21
    k_out[e(1), e(2)] = k21.T
    k_out[e(2), e(0)] = k20
    k_out[e(0), e(2)] = k20.T
    k_out[e(1), e(1)] = k11
    k_out[e(1), e(0)] = k10
    k_out[e(0), e(1)] = k10.T
    k_out[e(0), e(0)] = k00


def left_kernel(k_ref, p_ref, out, k3):
    @pl.when(pl.program_id(0) == 0)
    def _():
        k3[...] = right3(k_ref[...])

    n = p_ref.shape[1]
    hi, lo = split(dot3k(left3(p_ref[...]), k3[...]))
    out[:, :n] = hi
    out[:, n:] = lo


def final_kernel(n_row, ids, w_ref, t_ref, zm, ym, zo, yo, m_mine, m_other, s0, s1, s2, g, g21, out, loss, ws, hi, lo, obuf, in_sems, out_sems):
    local, cols = w_ref.shape
    n_z, s = zm.shape[0], zm.shape[1]
    width = cols // 2
    tile = obuf.shape[1]
    n_tile = local // tile
    idx = lax.axis_index("row")
    core, chip = idx & 1, idx >> 1
    c_f, c_l, c_m, mid_block = positions(n_row, local, ids)
    n = PICKS * BLOCK
    mine_at = jnp.where(core == 0, c_f, c_l) * BLOCK
    other_at = jnp.where(core == 0, c_l, c_f) * BLOCK

    def line_copies(h):
        cs = slice(h * width, (h + 1) * width)
        made = []
        for k in range(n_z):
            for j, (y, at, ref) in enumerate(((0, mine_at, zm), (1, mine_at, ym), (0, other_at, zo), (1, other_at, yo))):
                row = pl.multiple_of(at + (chip ^ (2 * k + y)) * s, SUB)
                made.append(pltpu.make_async_copy(ref.at[k, :, cs], ws.at[pl.ds(row, s), cs], in_sems.at[h, 4 * k + j]))
        return made

    def mid_copies(h):
        cs = slice(h * width, (h + 1) * width)
        made = []
        for k in range(2 * n_z):
            row = pl.multiple_of(c_m * BLOCK + (chip ^ k) * s, SUB)
            made.append((ws.at[pl.ds(row, s), cs], k, in_sems.at[h, 4 * n_z + k]))
        return made

    for h in range(2):
        for c in line_copies(h):
            c.start()
        for side, ref in ((0, m_mine), (1, m_other)):

            @pl.when((core ^ h) == side)
            def _():
                for dst, k, sem in mid_copies(h):
                    pltpu.make_async_copy(ref.at[k], dst, sem).start()

    def store(at):
        row, col = (at % n_tile) * tile, (at // n_tile) * width
        if not isinstance(at, int):
            row, col = pl.multiple_of(row, SUB), pl.multiple_of(col, LANES)
        dst = out.at[pl.ds(row, tile), pl.ds(col, width)]
        return pltpu.make_async_copy(obuf.at[at & 1], dst, out_sems.at[at & 1])

    totals = [jnp.zeros((SUB, LANES), F32) for _ in range(PICKS)]
    e = lambda i: slice(i * BLOCK, (i + 1) * BLOCK)
    for h in range(2):
        cs = slice(h * width, (h + 1) * width)
        for c in line_copies(h):
            c.wait()
        for dst, k, sem in mid_copies(h):
            pltpu.make_async_copy(m_mine.at[k], dst, sem).wait()
        hi[:, cs], lo[:, cs] = split(ws[:, cs])

        def one_tile(r, _):
            at = h * n_tile + r
            rs = pl.ds(pl.multiple_of(r * tile, 2 * SUB), tile)
            top = hi[:, cs]
            prod = jnp.dot(t_ref[rs, :], jnp.concatenate([top, top], axis=0), preferred_element_type=F32)
            prod = prod + jnp.dot(t_ref[rs, :n], lo[:, cs], preferred_element_type=F32)

            @pl.when(at >= 2)
            def _():
                store(at - 2).wait()

            block_of = (idx * local + r * tile + lax.broadcasted_iota(jnp.int32, (tile, 1), 0)) // BLOCK
            listed = (block_of == 0) | (block_of == n_row * local // BLOCK - 1) | (block_of == mid_block)
            obuf[at & 1] = jnp.where(listed, 0.0, w_ref[rs, cs] - prod)
            store(at).start()
            return 0

        lax.fori_loop(0, n_tile, one_tile, 0)

        r0 = jnp.concatenate([hi[e(0), cs], lo[e(0), cs], hi[e(0), cs]], axis=0)
        v0 = ws[e(0), cs]
        v1 = ws[e(1), cs] - dot3k(left3(g[0]), r0)
        r1 = right3(v1)
        v2 = ws[e(2), cs] - dot3k(left3(g[1]), r0) - dot3k(left3(g21[...]), r1)
        for i, (v, r, inv) in enumerate(((v0, r0, s0), (v1, r1, s1), (v2, right3(v2), s2))):
            part = v * dot3k(left3(inv[...]), r)
            part = jnp.sum(part.reshape(BLOCK // SUB, SUB, width), axis=0)
            for j in range(width // LANES):
                totals[i] = totals[i] + part[:, j * LANES : (j + 1) * LANES]
    for i in range(PICKS):
        loss[i] = jnp.sum(totals[i]) * (1.0 / (2.0 * BLOCK * cols))
    for at in range(max(0, 2 * n_tile - 2), 2 * n_tile):
        store(at).wait()


VMEM = pl.BlockSpec(memory_space=pltpu.VMEM)
SMEM = pl.BlockSpec(memory_space=pltpu.SMEM)
ANY = pl.BlockSpec(memory_space=pl.ANY)
HBM = pl.BlockSpec(memory_space=pltpu.HBM)
def room(mib):
    return pltpu.CompilerParams(vmem_limit_bytes=mib << 20)


def shape(*dims, dtype=F32):
    return jax.ShapeDtypeStruct(dims, dtype)


def square(n):
    return shape(n, BLOCK, BLOCK)


HALVES = [pltpu.VMEM((HALF, HALF), F32), pltpu.VMEM((2, HALF, HALF), F32)]


def cost(us):
    return pl.CostEstimate(flops=int(us * 1e9), bytes_accessed=1 << 20, transcendentals=0)


def run_pack(n_row, picked, ids, src):
    local, cols = src.shape
    width = (BLOCK if picked else cols) // 2
    grain = min(BLOCK, local & -local)
    half = shape(BLOCK, width)
    return pl.pallas_call(
        functools.partial(pack_kernel, n_row, picked),
        out_shape=(shape(BLOCK, cols), half, half),
        in_specs=[SMEM, HBM],
        out_specs=(VMEM, VMEM, VMEM),
        scratch_shapes=[pltpu.SemaphoreType.DMA((1 + 2 * (BLOCK // grain),))],
        compiler_params=room(8),
        name="pack_panels" if picked else "pack_weights",
    )(ids, pltpu.with_memory_space_constraint(src, pltpu.HBM))


def run_first(n_row, local, ids, mine, other):
    return pl.pallas_call(
        functools.partial(first_kernel, n_row, local),
        out_shape=(shape(BLOCK, BLOCK), square(2), square(3)),
        in_specs=[SMEM, VMEM, VMEM],
        out_specs=(VMEM, VMEM, VMEM),
        scratch_shapes=[
            pltpu.VMEM((2, BLOCK, PICKS * BLOCK), F32),
            pltpu.VMEM((2, BLOCK, HALF), F32),
            pltpu.VMEM((PICKS, PICKS, BLOCK, BLOCK), F32),
        ]
        + HALVES,
        compiler_params=room(16),
        cost_estimate=cost(13),
        name="first_pick",
    )(ids, mine, other)


def run_second(a):
    one = shape(BLOCK, BLOCK)
    return pl.pallas_call(
        second_kernel,
        out_shape=(one, one, one),
        in_specs=[VMEM],
        out_specs=(VMEM,) * 3,
        scratch_shapes=HALVES,
        compiler_params=room(10),
        cost_estimate=cost(12),
        name="second_pick",
    )(a)


def run_third(*args):
    n = PICKS * BLOCK
    return pl.pallas_call(
        third_kernel,
        out_shape=(shape(BLOCK, BLOCK), shape(n, n)),
        in_specs=[VMEM] * 5,
        out_specs=(VMEM,) * 2,
        scratch_shapes=HALVES,
        compiler_params=room(14),
        cost_estimate=cost(14),
        name="third_pick",
    )(*args)


def tile_of(rows):
    return max(t for t in range(SUB, 2 * BLOCK + 1, SUB) if rows % t == 0)


def run_left(k, panels):
    rows, n = panels.shape
    tile = tile_of(rows)
    return pl.pallas_call(
        left_kernel,
        grid=(rows // tile,),
        out_shape=shape(rows, 2 * n, dtype=BF16),
        in_specs=[VMEM, pl.BlockSpec((tile, n), lambda i: (i, 0))],
        out_specs=pl.BlockSpec((tile, 2 * n), lambda i: (i, 0)),
        scratch_shapes=[pltpu.VMEM((3 * n, n), BF16)],
        compiler_params=room(24),
        cost_estimate=cost(10),
        name="left_factor",
    )(k, panels)


def run_final(n_row, ids, weights, t, zm, ym, zo, yo, m_mine, m_other, s0, s1, s2, g, g21):
    rows, cols = weights.shape
    n = PICKS * BLOCK
    n_z = zm.shape[0]
    return pl.pallas_call(
        functools.partial(final_kernel, n_row),
        out_shape=(shape(rows, cols), shape(PICKS)),
        in_specs=[SMEM, VMEM, VMEM] + [ANY] * 6 + [VMEM] * 5,
        out_specs=(ANY, SMEM),
        scratch_shapes=[
            pltpu.VMEM((n, cols), F32),
            pltpu.VMEM((n, cols), BF16),
            pltpu.VMEM((n, cols), BF16),
            pltpu.VMEM((2, tile_of(rows), cols // 2), F32),
            pltpu.SemaphoreType.DMA((2, 6 * n_z)),
            pltpu.SemaphoreType.DMA((2,)),
        ],
        compiler_params=room(28),
        cost_estimate=cost(18),
        name="final_update",
    )(ids, weights, t, zm, ym, zo, yo, m_mine, m_other, s0, s1, s2, g, g21)


def body(n_row, panels, weights, block_ids):
    local, cols = weights.shape
    n_chip = n_row // 2
    s = BLOCK // n_chip
    idx = lax.axis_index("row")
    core, chip = idx & 1, idx >> 1
    last = n_row - 1

    def swap(x, bit):
        return lax.ppermute(x, "row", [(i, i ^ bit) for i in range(n_row)])

    def parts(x, bit_value):
        half = x.shape[0] // 2
        keep = lax.dynamic_slice_in_dim(x, bit_value * half, half, 0)
        return keep, lax.dynamic_slice_in_dim(x, (1 - bit_value) * half, half, 0)

    from_root = jnp.where(core == 0, chip, n_chip - 1 - chip)

    def scatter(x):
        bit = n_chip // 2
        while bit:
            keep, send = parts(x, (chip // bit) & 1)
            pairs = []
            for c in range(0, n_chip, 2 * bit):
                pairs += [(2 * c, 2 * (c + bit)), (last - 2 * c, last - 2 * (c + bit))]
            got = lax.ppermute(send, "row", pairs)
            x = jnp.where(from_root % (2 * bit) == bit, got, keep)
            bit //= 2
        return x

    def halve_core(keep, send):
        return (keep + swap(send, 1)).reshape(n_chip, s, keep.shape[1])

    def halve_step(x, bit):
        half = x.reshape(x.shape[0] // 2, 2, s, x.shape[2])
        mine = (chip // bit) & 1
        keep = lax.dynamic_index_in_dim(half, mine, 1, keepdims=False)
        send = lax.dynamic_index_in_dim(half, 1 - mine, 1, keepdims=False)
        return keep + swap(send, 2 * bit)

    def halve(x, bits):
        for bit in bits:
            x = halve_step(x, bit)
        return x

    tie = lax.optimization_barrier
    n_z = n_chip // 2
    bits = [1 << i for i in range(n_chip.bit_length() - 1)]

    a_block, a_keep, a_send = run_pack(n_row, True, block_ids, panels)
    a_mid = halve(halve_core(a_keep, a_send), bits)
    a_own = jnp.concatenate([scatter(a_block), a_mid.reshape(s, -1)], axis=1)

    w_block, w_keep, w_send = run_pack(n_row, False, block_ids, weights)
    w_mid = halve_core(w_keep, w_send)
    a_own, w_mid = tie((a_own, w_mid))
    w_line = scatter(w_block)
    a_mine = jnp.stack([a_own] + [swap(a_own, 2 * k) for k in range(1, n_chip)])
    w_mid = halve_step(w_mid, bits[0])
    a_mine, w_mid, w_line = tie((a_mine, w_mid, w_line))
    a_other = swap(a_mine, 1)
    w_mid = halve(w_mid, bits[1:-1])
    a_other, w_mid = tie((a_other, w_mid))

    f_z = [w_line] + [swap(w_line, 4 * k) for k in range(1, n_z)]
    w_mid = halve(w_mid, bits[-1:]).reshape(s, -1)
    s0, g, a1 = run_first(n_row, local, block_ids, a_mine, a_other)
    a1, w_mid = tie((a1, w_mid))
    m_y = swap(w_mid, 2)
    s1, g21, a2 = run_second(a1)
    a2, m_y, *f_z = tie((a2, m_y, *f_z))
    m_parts = jnp.stack([w_mid, m_y])
    m_z = [m_parts] + [swap(m_parts, 4 * k) for k in range(1, n_z)]
    zm = jnp.stack(f_z)
    ym = swap(zm, 2)
    zo = swap(zm, 1)
    s2, k = run_third(a2, s0, s1, g, g21)
    t = run_left(k, panels)
    t, ym, zo, *m_z = tie((t, ym, zo, *m_z))
    m_mine = jnp.concatenate(m_z, axis=0)
    m_other = swap(m_mine, 1)
    yo = swap(ym, 1)
    return run_final(n_row, block_ids, weights, t, zm, ym, zo, yo, m_mine, m_other, s0, s1, s2, g, g21)


def solution(mesh):
    n_row = mesh.shape["row"]
    rows = P(("groups", "row"), None)
    return jax.shard_map(
        functools.partial(body, n_row),
        mesh=mesh,
        in_specs=(rows, rows, P("groups")),
        out_specs=(rows, P("groups")),
        check_vma=False,
    )
```

```python
import functools

import jax
import jax.numpy as jnp
from jax import lax
from jax.experimental import pallas as pl
from jax.experimental.pallas import tpu as pltpu
from jax.sharding import PartitionSpec as P

BLOCK = 256
PICKS = 3
HALF = BLOCK // 2
SUB = 8
LANES = 128
EXACT = lax.Precision.HIGHEST
F32 = jnp.float32
BF16 = jnp.bfloat16


def mm(a, b):
    return lax.dot_general(a, b, (((1,), (0,)), ((), ())), precision=EXACT, preferred_element_type=F32)


def mm_nt(a, b):
    return lax.dot_general(a, b, (((1,), (1,)), ((), ())), precision=EXACT, preferred_element_type=F32)


def mm_tn(a, b):
    return lax.dot_general(a, b, (((0,), (0,)), ((), ())), precision=EXACT, preferred_element_type=F32)


def lane_bcast(x, c):
    return jnp.broadcast_to(x[:, c : c + 1], (SUB, LANES))


def row_bcast(x, j):
    return jnp.broadcast_to(x[j : j + 1, :], (SUB, LANES))


def inv_half(m):
    n_panels = HALF // SUB
    rows = [m[SUB * i : SUB * i + SUB, :] for i in range(n_panels)]
    lane = lax.broadcasted_iota(jnp.int32, (SUB, LANES), 1)
    sub = lax.broadcasted_iota(jnp.int32, (SUB, LANES), 0)
    for p in range(n_panels):
        panel = rows[p]
        cols = [lane_bcast(panel, SUB * p + k) for k in range(SUB)]
        for j in range(SUB):
            is_j = sub == j
            r = 1.0 / row_bcast(cols[j], j)
            f = cols[j] * r
            panel = jnp.where(lane == SUB * p + j, jnp.where(is_j, 1.0, 0.0), panel)
            u = row_bcast(panel, j)
            panel = jnp.where(is_j, u * r, panel - f * u)
            for k in range(j + 1, SUB):
                uk = row_bcast(cols[k], j)
                cols[k] = jnp.where(is_j, uk * r, cols[k] - f * uk)
        reps = [row_bcast(panel, k) for k in range(SUB)]
        in_panel = (lane >= SUB * p) & (lane < SUB * p + SUB)
        for step in range(1, n_panels):
            i = (p + step) % n_panels
            t = [lane_bcast(rows[i], SUB * p + k) * reps[k] for k in range(SUB)]
            total = ((t[0] + t[1]) + (t[2] + t[3])) + ((t[4] + t[5]) + (t[6] + t[7]))
            rows[i] = jnp.where(in_panel, 0.0, rows[i]) - total
        rows[p] = panel
    return jnp.concatenate(rows, axis=0)


def inv_block(ref, half_in, half_out):
    def one(h, _):
        @pl.when(h == 0)
        def _():
            half_in[...] = ref[:HALF, :HALF]

        @pl.when(h == 1)
        def _():
            c = ref[HALF:, :HALF]
            half_in[...] = ref[HALF:, HALF:] - mm_nt(mm(c, half_out[0]), c)

        half_out[h] = inv_half(half_in[...])
        return 0

    lax.fori_loop(0, 2, one, 0)
    ai, si = half_out[0], half_out[1]
    g = mm(ref[HALF:, :HALF], ai)
    h = mm(si, g)
    top = jnp.concatenate([ai + mm_tn(g, h), -h.T], axis=1)
    return jnp.concatenate([top, jnp.concatenate([-h, si], axis=1)], axis=0)


def split(x):
    hi = x.astype(BF16)
    return hi, (x - hi.astype(F32)).astype(BF16)


def dot3k(stacked_left, stacked_right):
    return jnp.dot(stacked_left, stacked_right, preferred_element_type=F32)


def left3(x):
    hi, lo = split(x)
    return jnp.concatenate([hi, hi, lo], axis=1)


def right3(x):
    hi, lo = split(x)
    return jnp.concatenate([hi, lo, hi], axis=0)


def positions(n_row, local, ids):
    last_block = n_row * local // BLOCK - 1
    at = lambda v: jnp.where(ids[0] == v, 0, jnp.where(ids[1] == v, 1, 2)).astype(jnp.int32)
    c_f, c_l = at(0), at(last_block)
    return c_f, c_l, PICKS - c_f - c_l, ids[0] + ids[1] + ids[2] - last_block


def pack_kernel(n_row, picked, ids, src, line_out, keep_out, send_out, sems):
    local, cols = src.shape
    idx = lax.axis_index("row")
    core = idx & 1
    _, _, c_m, mid = positions(n_row, local, ids)
    grain = min(BLOCK, local & -local)
    width = keep_out.shape[1]
    base = jnp.where(idx == n_row - 1, local - BLOCK, 0)
    line = pltpu.make_async_copy(src.at[pl.ds(pl.multiple_of(base, SUB), BLOCK), :], line_out, sems.at[0])
    line.start()
    left = c_m * BLOCK if picked else 0

    def copy(i, out, side, sem):
        row = pl.multiple_of(mid * BLOCK + i * grain - idx * local, SUB)
        at = src.at[pl.ds(row, grain), pl.ds(pl.multiple_of(left + side * width, LANES), width)]
        return pltpu.make_async_copy(at, out.at[pl.ds(i * grain, grain), :], sem)

    def each(act):
        for i in range(BLOCK // grain):
            row = mid * BLOCK + i * grain - idx * local
            owned = (row >= 0) & (row < local)
            for j, (out, side) in enumerate(((keep_out, core), (send_out, 1 - core))):
                act(i, out, side, sems.at[1 + 2 * i + j], owned)

    def begin(i, out, side, sem, owned):
        @pl.when(owned)
        def _():
            copy(i, out, side, sem).start()

        @pl.when(jnp.logical_not(owned))
        def _():
            out[i * grain : (i + 1) * grain, :] = jnp.zeros((grain, width), F32)

    def finish(i, out, side, sem, owned):
        @pl.when(owned)
        def _():
            copy(i, out, side, sem).wait()

    each(begin)
    each(finish)
    line.wait()


def first_kernel(n_row, local, ids, mine, other, s_out, g_out, a_out, fl, mid, blk, half_in, half_out):
    idx = lax.axis_index("row")
    core = idx & 1
    c_f, c_l, c_m, _ = positions(n_row, local, ids)
    width = PICKS * BLOCK
    for at, ref in ((core, mine), (1 - core, other)):
        fl[at] = ref[:, :width]
        mid[at] = ref[:, width:]
    for j in range(PICKS):
        blk[c_f, j] = fl[0, :, j * BLOCK : (j + 1) * BLOCK]
        blk[c_l, j] = fl[1, :, j * BLOCK : (j + 1) * BLOCK]
    blk[c_m, c_f] = blk[c_f, c_m].T
    blk[c_m, c_l] = blk[c_l, c_m].T
    blk[c_m, c_m, :, :HALF] = mid[0]
    blk[c_m, c_m, :, HALF:] = mid[1]
    s0 = inv_block(blk.at[0, 0], half_in, half_out)
    s_out[...] = s0
    a10, a20 = blk[1, 0], blk[2, 0]
    g10, g20 = mm(a10, s0), mm(a20, s0)
    g_out[0] = g10
    g_out[1] = g20
    a_out[0] = blk[1, 1] - mm_nt(g10, a10)
    a_out[1] = blk[2, 1] - mm_nt(g20, a10)
    a_out[2] = blk[2, 2] - mm_nt(g20, a20)


def second_kernel(a_in, s_out, g_out, a_out, half_in, half_out):
    s1 = inv_block(a_in.at[0], half_in, half_out)
    s_out[...] = s1
    a21 = a_in[1]
    g21 = mm(a21, s1)
    g_out[...] = g21
    a_out[...] = a_in[2] - mm_nt(g21, a21)


def third_kernel(a_in, s0, s1, g, g21, s_out, k_out, half_in, half_out):
    s2 = inv_block(a_in, half_in, half_out)
    s_out[...] = s2
    g10, g20 = g[0], g[1]
    j21 = -g21[...]
    j20 = mm(g21[...], g10) - g20
    k21, k20 = mm(s2, j21), mm(s2, j20)
    t10 = mm(s1[...], g10)
    k11 = s1[...] + mm_tn(j21, k21)
    k10 = mm_tn(j21, k20) - t10
    k00 = s0[...] + mm_tn(g10, t10) + mm_tn(j20, k20)
    e = lambda i: slice(i * BLOCK, (i + 1) * BLOCK)
    k_out[e(2), e(2)] = s2
    k_out[e(2), e(1)] = k21
    k_out[e(1), e(2)] = k21.T
    k_out[e(2), e(0)] = k20
    k_out[e(0), e(2)] = k20.T
    k_out[e(1), e(1)] = k11
    k_out[e(1), e(0)] = k10
    k_out[e(0), e(1)] = k10.T
    k_out[e(0), e(0)] = k00


def left_kernel(k_ref, p_ref, out, k3):
    @pl.when(pl.program_id(0) == 0)
    def _():
        k3[...] = right3(k_ref[...])

    n = p_ref.shape[1]
    hi, lo = split(dot3k(left3(p_ref[...]), k3[...]))
    out[:, :n] = hi
    out[:, n:] = lo


def final_kernel(n_row, ids, w_ref, t_ref, fl_mine, fl_other, m_mine, m_other, s0, s1, s2, g, g21, out, loss, ws, hi, lo, obuf, in_sems, out_sems):
    local, cols = w_ref.shape
    n_chip, s = m_mine.shape[0], m_mine.shape[1]
    width = cols // 2
    tile = obuf.shape[1]
    n_tile = local // tile
    idx = lax.axis_index("row")
    core, chip = idx & 1, idx >> 1
    c_f, c_l, c_m, mid_block = positions(n_row, local, ids)
    n = PICKS * BLOCK

    def line_copies(h):
        cs = slice(h * width, (h + 1) * width)
        made = []
        for j, (at, ref) in enumerate(((jnp.where(core == 0, c_f, c_l), fl_mine), (jnp.where(core == 0, c_l, c_f), fl_other))):
            row = pl.multiple_of(at * BLOCK, BLOCK)
            made.append(pltpu.make_async_copy(ref.at[:, cs], ws.at[pl.ds(row, BLOCK), cs], in_sems.at[h, n_chip + j]))
        return made

    def mid_copies(h):
        cs = slice(h * width, (h + 1) * width)
        made = []
        for k in range(n_chip):
            row = pl.multiple_of(c_m * BLOCK + (chip ^ k) * s, SUB)
            made.append((ws.at[pl.ds(row, s), cs], k, in_sems.at[h, k]))
        return made

    for h in range(2):
        for c in line_copies(h):
            c.start()
        for side, ref in ((0, m_mine), (1, m_other)):

            @pl.when((core ^ h) == side)
            def _():
                for dst, k, sem in mid_copies(h):
                    pltpu.make_async_copy(ref.at[k], dst, sem).start()

    def store(at):
        row, col = (at % n_tile) * tile, (at // n_tile) * width
        if not isinstance(at, int):
            row, col = pl.multiple_of(row, SUB), pl.multiple_of(col, LANES)
        dst = out.at[pl.ds(row, tile), pl.ds(col, width)]
        return pltpu.make_async_copy(obuf.at[at & 1], dst, out_sems.at[at & 1])

    totals = [jnp.zeros((SUB, LANES), F32) for _ in range(PICKS)]
    e = lambda i: slice(i * BLOCK, (i + 1) * BLOCK)
    for h in range(2):
        cs = slice(h * width, (h + 1) * width)
        for c in line_copies(h):
            c.wait()
        for dst, k, sem in mid_copies(h):
            pltpu.make_async_copy(m_mine.at[k], dst, sem).wait()
        hi[:, cs], lo[:, cs] = split(ws[:, cs])

        def one_tile(r, _):
            at = h * n_tile + r
            rs = pl.ds(pl.multiple_of(r * tile, 2 * SUB), tile)
            top = hi[:, cs]
            prod = jnp.dot(t_ref[rs, :], jnp.concatenate([top, top], axis=0), preferred_element_type=F32)
            prod = prod + jnp.dot(t_ref[rs, :n], lo[:, cs], preferred_element_type=F32)

            @pl.when(at >= 2)
            def _():
                store(at - 2).wait()

            block_of = (idx * local + r * tile + lax.broadcasted_iota(jnp.int32, (tile, 1), 0)) // BLOCK
            listed = (block_of == 0) | (block_of == n_row * local // BLOCK - 1) | (block_of == mid_block)
            obuf[at & 1] = jnp.where(listed, 0.0, w_ref[rs, cs] - prod)
            store(at).start()
            return 0

        lax.fori_loop(0, n_tile, one_tile, 0)

        r0 = jnp.concatenate([hi[e(0), cs], lo[e(0), cs], hi[e(0), cs]], axis=0)
        v0 = ws[e(0), cs]
        v1 = ws[e(1), cs] - dot3k(left3(g[0]), r0)
        r1 = right3(v1)
        v2 = ws[e(2), cs] - dot3k(left3(g[1]), r0) - dot3k(left3(g21[...]), r1)
        for i, (v, r, inv) in enumerate(((v0, r0, s0), (v1, r1, s1), (v2, right3(v2), s2))):
            part = v * dot3k(left3(inv[...]), r)
            part = jnp.sum(part.reshape(BLOCK // SUB, SUB, width), axis=0)
            for j in range(width // LANES):
                totals[i] = totals[i] + part[:, j * LANES : (j + 1) * LANES]
    for i in range(PICKS):
        loss[i] = jnp.sum(totals[i]) * (1.0 / (2.0 * BLOCK * cols))
    for at in range(max(0, 2 * n_tile - 2), 2 * n_tile):
        store(at).wait()


VMEM = pl.BlockSpec(memory_space=pltpu.VMEM)
SMEM = pl.BlockSpec(memory_space=pltpu.SMEM)
ANY = pl.BlockSpec(memory_space=pl.ANY)
HBM = pl.BlockSpec(memory_space=pltpu.HBM)
def room(mib):
    return pltpu.CompilerParams(vmem_limit_bytes=mib << 20)


def shape(*dims, dtype=F32):
    return jax.ShapeDtypeStruct(dims, dtype)


def square(n):
    return shape(n, BLOCK, BLOCK)


HALVES = [pltpu.VMEM((HALF, HALF), F32), pltpu.VMEM((2, HALF, HALF), F32)]


def cost(us):
    return pl.CostEstimate(flops=int(us * 1e9), bytes_accessed=1 << 20, transcendentals=0)


def run_pack(n_row, picked, ids, src):
    local, cols = src.shape
    width = (BLOCK if picked else cols) // 2
    grain = min(BLOCK, local & -local)
    half = shape(BLOCK, width)
    return pl.pallas_call(
        functools.partial(pack_kernel, n_row, picked),
        out_shape=(shape(BLOCK, cols), half, half),
        in_specs=[SMEM, HBM],
        out_specs=(VMEM, VMEM, VMEM),
        scratch_shapes=[pltpu.SemaphoreType.DMA((1 + 2 * (BLOCK // grain),))],
        compiler_params=room(8),
        name="pack_panels" if picked else "pack_weights",
    )(ids, pltpu.with_memory_space_constraint(src, pltpu.HBM))


def run_first(n_row, local, ids, mine, other):
    return pl.pallas_call(
        functools.partial(first_kernel, n_row, local),
        out_shape=(shape(BLOCK, BLOCK), square(2), square(3)),
        in_specs=[SMEM, VMEM, VMEM],
        out_specs=(VMEM, VMEM, VMEM),
        scratch_shapes=[
            pltpu.VMEM((2, BLOCK, PICKS * BLOCK), F32),
            pltpu.VMEM((2, BLOCK, HALF), F32),
            pltpu.VMEM((PICKS, PICKS, BLOCK, BLOCK), F32),
        ]
        + HALVES,
        compiler_params=room(16),
        cost_estimate=cost(13),
        name="first_pick",
    )(ids, mine, other)


def run_second(a):
    one = shape(BLOCK, BLOCK)
    return pl.pallas_call(
        second_kernel,
        out_shape=(one, one, one),
        in_specs=[VMEM],
        out_specs=(VMEM,) * 3,
        scratch_shapes=HALVES,
        compiler_params=room(10),
        cost_estimate=cost(12),
        name="second_pick",
    )(a)


def run_third(*args):
    n = PICKS * BLOCK
    return pl.pallas_call(
        third_kernel,
        out_shape=(shape(BLOCK, BLOCK), shape(n, n)),
        in_specs=[VMEM] * 5,
        out_specs=(VMEM,) * 2,
        scratch_shapes=HALVES,
        compiler_params=room(14),
        cost_estimate=cost(14),
        name="third_pick",
    )(*args)


def tile_of(rows):
    return max(t for t in range(SUB, 2 * BLOCK + 1, SUB) if rows % t == 0)


def run_left(k, panels):
    rows, n = panels.shape
    tile = tile_of(rows)
    return pl.pallas_call(
        left_kernel,
        grid=(rows // tile,),
        out_shape=shape(rows, 2 * n, dtype=BF16),
        in_specs=[VMEM, pl.BlockSpec((tile, n), lambda i: (i, 0))],
        out_specs=pl.BlockSpec((tile, 2 * n), lambda i: (i, 0)),
        scratch_shapes=[pltpu.VMEM((3 * n, n), BF16)],
        compiler_params=room(24),
        cost_estimate=cost(10),
        name="left_factor",
    )(k, panels)


def run_final(n_row, ids, weights, t, fl_mine, fl_other, m_mine, m_other, s0, s1, s2, g, g21):
    rows, cols = weights.shape
    n = PICKS * BLOCK
    n_chip = m_mine.shape[0]
    return pl.pallas_call(
        functools.partial(final_kernel, n_row),
        out_shape=(shape(rows, cols), shape(PICKS)),
        in_specs=[SMEM, VMEM, VMEM] + [ANY] * 4 + [VMEM] * 5,
        out_specs=(ANY, SMEM),
        scratch_shapes=[
            pltpu.VMEM((n, cols), F32),
            pltpu.VMEM((n, cols), BF16),
            pltpu.VMEM((n, cols), BF16),
            pltpu.VMEM((2, tile_of(rows), cols // 2), F32),
            pltpu.SemaphoreType.DMA((2, n_chip + 2)),
            pltpu.SemaphoreType.DMA((2,)),
        ],
        compiler_params=room(28),
        cost_estimate=cost(18),
        name="final_update",
    )(ids, weights, t, fl_mine, fl_other, m_mine, m_other, s0, s1, s2, g, g21)


def body(n_row, panels, weights, block_ids):
    local, cols = weights.shape
    n_chip = n_row // 2
    n_z = n_chip // 2
    s = BLOCK // n_chip
    idx = lax.axis_index("row")
    core, chip = idx & 1, idx >> 1
    last = n_row - 1
    bits = [1 << i for i in range(n_chip.bit_length() - 1)]
    tie = lax.optimization_barrier

    def swap(x, bit):
        return lax.ppermute(x, "row", [(i, i ^ bit) for i in range(n_row)])

    place = jnp.where(core == 0, chip, n_chip - 1 - chip)
    place_y, place_z = place & 1, place >> 1

    def send(x, pairs):
        both = [(2 * a, 2 * b) for a, b in pairs] + [(last - 2 * a, last - 2 * b) for a, b in pairs]
        return lax.ppermute(x, "row", both)

    def tree_step(x, bit, done):
        holders = [c for c in range(n_chip) if c & ~done == 0]
        got = send(x, [(c, c | bit) for c in holders])
        is_target = ((place & ~(done | bit)) == 0) & ((place & bit) != 0)
        return jnp.where(is_target, got, x), done | bit

    def halve_step(x, bit):
        half = x.reshape(x.shape[0] // 2, 2, s, x.shape[2])
        mine = (chip // bit) & 1
        keep = lax.dynamic_index_in_dim(half, mine, 1, keepdims=False)
        give = lax.dynamic_index_in_dim(half, 1 - mine, 1, keepdims=False)
        return keep + swap(give, 2 * bit)

    a_block, a_keep, a_give = run_pack(n_row, True, block_ids, panels)
    orders = ([bits[-1], bits[0]] + bits[1:-1][::-1], [bits[0], bits[-1]] + bits[1:-1][::-1])
    halves = [a_block[:HALF], a_block[HALF:]]
    done = [0, 0]
    for t in range(len(bits)):
        for i in range(2):
            halves[i], done[i] = tree_step(halves[i], orders[i][t], done[i])
    a_mid = a_keep + swap(a_give, 1)
    for bit in bits:
        a_mid = a_mid + swap(a_mid, 2 * bit)
    a_mine = jnp.concatenate([jnp.concatenate(halves, axis=0), a_mid], axis=1)

    w_block, w_keep, w_give = run_pack(n_row, False, block_ids, weights)
    top, bot = w_block[:HALF], w_block[HALF:]
    w_mid = (w_keep + swap(w_give, 1)).reshape(n_chip, s, cols // 2)
    w_mid = halve_step(w_mid, bits[0])

    def z_pairs(z, ys):
        return [(2 * z + y, 2 * (z + 1) + y) for y in ys]

    top_got = send(top, z_pairs(0, [0]))
    bot_got = send(bot, [(0, 1)])
    bot = jnp.where(place == 1, bot_got, bot)
    top = jnp.where(place_z == 1, top_got, top)
    for bit in bits[1:]:
        w_mid = halve_step(w_mid, bit)
    w_mid = w_mid.reshape(s, cols // 2)
    a_other = swap(a_mine, 1)
    a_other, w_mid, top_got, bot = tie((a_other, w_mid, top_got, bot))

    m_y = swap(w_mid, 2)

    def chain_step(z, top, top_got, bot, bot_send):
        bot_got = send(bot_send, z_pairs(z - 1, [0, 1]))
        if z < n_z - 1:
            top_got = send(top_got, z_pairs(z, [0]))
            top = jnp.where(place_z == z + 1, top_got, top)
        else:
            top_got = send(top, [(2 * c, 2 * c + 1) for c in range(n_z)])
            top = jnp.where(place_y == 1, top_got, top)
        bot = jnp.where(place_z == z, bot_got, bot)
        return top, top_got, bot, bot_got

    state = (top, top_got, bot, bot)
    state = chain_step(1, *state)
    s0, g, a1 = run_first(n_row, local, block_ids, a_mine, a_other)
    a1, m_y, *state = tie((a1, m_y, *state))
    m_parts = jnp.stack([w_mid, m_y])
    m_z = [m_parts] + [swap(m_parts, 4 * k) for k in range(1, n_z)]
    for z in range(2, n_z - 1):
        state = chain_step(z, *state)
    s1, g21, a2 = run_second(a1)
    a2, *state = tie((a2, *state))
    top, _, bot, _ = chain_step(n_z - 1, *state)
    s2, k = run_third(a2, s0, s1, g, g21)
    k, top, bot, *m_z = tie((k, top, bot, *m_z))
    fl_mine = jnp.concatenate([top, bot], axis=0)
    m_mine = jnp.concatenate(m_z, axis=0)
    fl_other = swap(fl_mine, 1)
    m_other = swap(m_mine, 1)
    t = run_left(k, panels)
    return run_final(n_row, block_ids, weights, t, fl_mine, fl_other, m_mine, m_other, s0, s1, s2, g, g21)


def solution(mesh):
    n_row = mesh.shape["row"]
    rows = P(("groups", "row"), None)
    return jax.shard_map(
        functools.partial(body, n_row),
        mesh=mesh,
        in_specs=(rows, rows, P("groups")),
        out_specs=(rows, P("groups")),
        check_vma=False,
    )
```

```python
import functools

import jax
import jax.numpy as jnp
from jax import lax
from jax.experimental import pallas as pl
from jax.experimental.pallas import tpu as pltpu
from jax.sharding import PartitionSpec as P

BLOCK = 256
PICKS = 3
HALF = BLOCK // 2
SUB = 8
LANES = 128
EXACT = lax.Precision.HIGHEST
F32 = jnp.float32
BF16 = jnp.bfloat16


def mm(a, b):
    return lax.dot_general(a, b, (((1,), (0,)), ((), ())), precision=EXACT, preferred_element_type=F32)


def mm_nt(a, b):
    return lax.dot_general(a, b, (((1,), (1,)), ((), ())), precision=EXACT, preferred_element_type=F32)


def mm_tn(a, b):
    return lax.dot_general(a, b, (((0,), (0,)), ((), ())), precision=EXACT, preferred_element_type=F32)


def lane_bcast(x, c):
    return jnp.broadcast_to(x[:, c : c + 1], (SUB, LANES))


def row_bcast(x, j):
    return jnp.broadcast_to(x[j : j + 1, :], (SUB, LANES))


def inv_half(m):
    n_panels = HALF // SUB
    rows = [m[SUB * i : SUB * i + SUB, :] for i in range(n_panels)]
    lane = lax.broadcasted_iota(jnp.int32, (SUB, LANES), 1)
    sub = lax.broadcasted_iota(jnp.int32, (SUB, LANES), 0)
    for p in range(n_panels):
        panel = rows[p]
        cols = [lane_bcast(panel, SUB * p + k) for k in range(SUB)]
        for j in range(SUB):
            is_j = sub == j
            r = 1.0 / row_bcast(cols[j], j)
            f = cols[j] * r
            panel = jnp.where(lane == SUB * p + j, jnp.where(is_j, 1.0, 0.0), panel)
            u = row_bcast(panel, j)
            panel = jnp.where(is_j, u * r, panel - f * u)
            for k in range(j + 1, SUB):
                uk = row_bcast(cols[k], j)
                cols[k] = jnp.where(is_j, uk * r, cols[k] - f * uk)
        reps = [row_bcast(panel, k) for k in range(SUB)]
        in_panel = (lane >= SUB * p) & (lane < SUB * p + SUB)
        for step in range(1, n_panels):
            i = (p + step) % n_panels
            t = [lane_bcast(rows[i], SUB * p + k) * reps[k] for k in range(SUB)]
            total = ((t[0] + t[1]) + (t[2] + t[3])) + ((t[4] + t[5]) + (t[6] + t[7]))
            rows[i] = jnp.where(in_panel, 0.0, rows[i]) - total
        rows[p] = panel
    return jnp.concatenate(rows, axis=0)


def inv_block(ref, half_in, half_out):
    def one(h, _):
        @pl.when(h == 0)
        def _():
            half_in[...] = ref[:HALF, :HALF]

        @pl.when(h == 1)
        def _():
            c = ref[HALF:, :HALF]
            half_in[...] = ref[HALF:, HALF:] - mm_nt(mm(c, half_out[0]), c)

        half_out[h] = inv_half(half_in[...])
        return 0

    lax.fori_loop(0, 2, one, 0)
    ai, si = half_out[0], half_out[1]
    g = mm(ref[HALF:, :HALF], ai)
    h = mm(si, g)
    top = jnp.concatenate([ai + mm_tn(g, h), -h.T], axis=1)
    return jnp.concatenate([top, jnp.concatenate([-h, si], axis=1)], axis=0)


def split(x):
    hi = x.astype(BF16)
    return hi, (x - hi.astype(F32)).astype(BF16)


def dot3k(stacked_left, stacked_right):
    return jnp.dot(stacked_left, stacked_right, preferred_element_type=F32)


def left3(x):
    hi, lo = split(x)
    return jnp.concatenate([hi, hi, lo], axis=1)


def right3(x):
    hi, lo = split(x)
    return jnp.concatenate([hi, lo, hi], axis=0)


def apply2(left, right):
    both = jnp.dot(jnp.concatenate(split(left), axis=0), right, preferred_element_type=F32)
    return both[:BLOCK] + both[BLOCK:]


def apply3(left, right_hi, right_lo):
    return apply2(left, right_hi) + jnp.dot(left.astype(BF16), right_lo, preferred_element_type=F32)


def positions(n_row, local, ids):
    last_block = n_row * local // BLOCK - 1
    at = lambda v: jnp.where(ids[0] == v, 0, jnp.where(ids[1] == v, 1, 2)).astype(jnp.int32)
    c_f, c_l = at(0), at(last_block)
    return c_f, c_l, PICKS - c_f - c_l, ids[0] + ids[1] + ids[2] - last_block


def pack_kernel(n_row, picked, ids, src, line_out, keep_out, send_out, sems):
    local, cols = src.shape
    idx = lax.axis_index("row")
    core = idx & 1
    _, _, c_m, mid = positions(n_row, local, ids)
    grain = min(BLOCK, local & -local)
    width = keep_out.shape[1]
    base = jnp.where(idx == n_row - 1, local - BLOCK, 0)
    line = pltpu.make_async_copy(src.at[pl.ds(pl.multiple_of(base, SUB), BLOCK), :], line_out, sems.at[0])
    line.start()
    left = c_m * BLOCK if picked else 0

    def copy(i, out, side, sem):
        row = pl.multiple_of(mid * BLOCK + i * grain - idx * local, SUB)
        at = src.at[pl.ds(row, grain), pl.ds(pl.multiple_of(left + side * width, LANES), width)]
        return pltpu.make_async_copy(at, out.at[pl.ds(i * grain, grain), :], sem)

    def each(act):
        for i in range(BLOCK // grain):
            row = mid * BLOCK + i * grain - idx * local
            owned = (row >= 0) & (row < local)
            for j, (out, side) in enumerate(((keep_out, core), (send_out, 1 - core))):
                act(i, out, side, sems.at[1 + 2 * i + j], owned)

    def begin(i, out, side, sem, owned):
        @pl.when(owned)
        def _():
            copy(i, out, side, sem).start()

        @pl.when(jnp.logical_not(owned))
        def _():
            out[i * grain : (i + 1) * grain, :] = jnp.zeros((grain, width), F32)

    def finish(i, out, side, sem, owned):
        @pl.when(owned)
        def _():
            copy(i, out, side, sem).wait()

    each(begin)
    each(finish)
    line.wait()


def first_kernel(n_row, local, ids, mine, other, s_out, g_out, a_out, fl, mid, blk, half_in, half_out):
    idx = lax.axis_index("row")
    core, chip = idx % 2, idx // 2
    c_f, c_l, c_m, _ = positions(n_row, local, ids)
    n_chip, s = mine.shape[0], mine.shape[1]
    width = PICKS * BLOCK
    for k in range(n_chip):
        row = pl.multiple_of((chip ^ k) * s, SUB)
        fl[core, pl.ds(row, s), :] = mine[k, :, :width]
        mid[core, pl.ds(row, s), :] = mine[k, :, width:]
        fl[1 - core, pl.ds(row, s), :] = other[k, :, :width]
        mid[1 - core, pl.ds(row, s), :] = other[k, :, width:]
    for j in range(PICKS):
        blk[c_f, j] = fl[0, :, j * BLOCK : (j + 1) * BLOCK]
        blk[c_l, j] = fl[1, :, j * BLOCK : (j + 1) * BLOCK]
    blk[c_m, c_f] = blk[c_f, c_m].T
    blk[c_m, c_l] = blk[c_l, c_m].T
    blk[c_m, c_m, :, :HALF] = mid[0]
    blk[c_m, c_m, :, HALF:] = mid[1]
    s0 = inv_block(blk.at[0, 0], half_in, half_out)
    s_out[...] = s0
    a10, a20 = blk[1, 0], blk[2, 0]
    g10, g20 = mm(a10, s0), mm(a20, s0)
    g_out[0] = g10
    g_out[1] = g20
    a_out[0] = blk[1, 1] - mm_nt(g10, a10)
    a_out[1] = blk[2, 1] - mm_nt(g20, a10)
    a_out[2] = blk[2, 2] - mm_nt(g20, a20)


def second_kernel(a_in, s_out, g_out, a_out, half_in, half_out):
    s1 = inv_block(a_in.at[0], half_in, half_out)
    s_out[...] = s1
    a21 = a_in[1]
    g21 = mm(a21, s1)
    g_out[...] = g21
    a_out[...] = a_in[2] - mm_nt(g21, a21)


def third_kernel(a_in, s0, s1, g, g21, s_out, k_out, half_in, half_out):
    s2 = inv_block(a_in, half_in, half_out)
    s_out[...] = s2
    g10, g20 = g[0], g[1]
    j21 = -g21[...]
    j20 = mm(g21[...], g10) - g20
    k21, k20 = mm(s2, j21), mm(s2, j20)
    t10 = mm(s1[...], g10)
    k11 = s1[...] + mm_tn(j21, k21)
    k10 = mm_tn(j21, k20) - t10
    k00 = s0[...] + mm_tn(g10, t10) + mm_tn(j20, k20)
    e = lambda i: slice(i * BLOCK, (i + 1) * BLOCK)
    k_out[e(2), e(2)] = s2
    k_out[e(2), e(1)] = k21
    k_out[e(1), e(2)] = k21.T
    k_out[e(2), e(0)] = k20
    k_out[e(0), e(2)] = k20.T
    k_out[e(1), e(1)] = k11
    k_out[e(1), e(0)] = k10
    k_out[e(0), e(1)] = k10.T
    k_out[e(0), e(0)] = k00


def left_kernel(k_ref, p_ref, out, k3):
    @pl.when(pl.program_id(0) == 0)
    def _():
        k3[...] = right3(k_ref[...])

    n = p_ref.shape[1]
    hi, lo = split(dot3k(left3(p_ref[...]), k3[...]))
    out[:, :n] = hi
    out[:, n:] = lo


def final_kernel(n_row, ids, w_ref, t_ref, zm, ym, zo, yo, m_mine, m_other, s0, s1, s2, g, g21, out, loss, ws, hi, lo, obuf, in_sems, out_sems):
    local, cols = w_ref.shape
    n_z, s = zm.shape[0], zm.shape[1]
    width = cols // 2
    tile = obuf.shape[1]
    n_tile = local // tile
    idx = lax.axis_index("row")
    core, chip = idx & 1, idx >> 1
    c_f, c_l, c_m, mid_block = positions(n_row, local, ids)
    n = PICKS * BLOCK
    first = min(cols, (width + BLOCK - 1) // BLOCK * BLOCK)
    chunks = (slice(0, first), slice(first, cols))
    mine_at = jnp.where(core == 0, c_f, c_l) * BLOCK
    other_at = jnp.where(core == 0, c_l, c_f) * BLOCK

    def line_copies(cs):
        made = []
        for k in range(n_z):
            for j, (y, at, ref) in enumerate(((0, mine_at, zm), (1, mine_at, ym), (0, other_at, zo), (1, other_at, yo))):
                row = pl.multiple_of(at + (chip ^ (2 * k + y)) * s, SUB)
                sem = in_sems.at[0 if cs.start == 0 else 1, 4 * k + j]
                made.append(pltpu.make_async_copy(ref.at[k, :, cs], ws.at[pl.ds(row, s), cs], sem))
        return made

    def mid_copies(side, ref):
        made = []
        for k in range(2 * n_z):
            row = pl.multiple_of(c_m * BLOCK + (chip ^ k) * s, SUB)
            dst = ws.at[pl.ds(row, s), slice(side * width, (side + 1) * width)]
            made.append(pltpu.make_async_copy(ref.at[k], dst, in_sems.at[side, 4 * n_z + k]))
        return made

    for side in range(2):
        for owner, ref in ((0, m_mine), (1, m_other)):

            @pl.when((core ^ side) == owner)
            def _():
                for c in mid_copies(side, ref):
                    c.start()

        for c in line_copies(chunks[side]):
            c.start()

    def store(h, r):
        cs = chunks[h]
        slot = r & 1
        row = r * tile if isinstance(r, int) else pl.multiple_of(r * tile, SUB)
        src = obuf.at[slot, :, slice(0, cs.stop - cs.start)]
        return pltpu.make_async_copy(src, out.at[pl.ds(row, tile), cs], out_sems.at[slot])

    totals = [jnp.zeros((SUB, LANES), F32) for _ in range(PICKS)]
    e = lambda i: slice(i * BLOCK, (i + 1) * BLOCK)
    for h, cs in enumerate(chunks):
        span = cs.stop - cs.start
        if h == 0:
            for side in range(2):
                for c in mid_copies(side, m_mine):
                    c.wait()
        for c in line_copies(cs):
            c.wait()
        top, low = split(ws[:, cs])
        hi[:n, cs] = top
        hi[n:, cs] = top
        lo[:, cs] = low

        def one_tile(r, _):
            rs = pl.ds(pl.multiple_of(r * tile, 2 * SUB), tile)
            prod = jnp.dot(t_ref[rs, :], hi[:, cs], preferred_element_type=F32)
            prod = prod + jnp.dot(t_ref[rs, :n], lo[:, cs], preferred_element_type=F32)

            @pl.when(r >= 2)
            def _():
                store(h, r - 2).wait()

            block_of = (idx * local + r * tile + lax.broadcasted_iota(jnp.int32, (tile, 1), 0)) // BLOCK
            listed = (block_of == 0) | (block_of == n_row * local // BLOCK - 1) | (block_of == mid_block)
            obuf[r & 1, :, :span] = jnp.where(listed, 0.0, w_ref[rs, cs] - prod)
            store(h, r).start()
            return 0

        lax.fori_loop(0, n_tile, one_tile, 0)

        v0, v0h, v0l = ws[e(0), cs], hi[e(0), cs], lo[e(0), cs]
        v1 = ws[e(1), cs] - apply3(g[0], v0h, v0l)
        v1h, v1l = split(v1)
        v2 = ws[e(2), cs] - apply3(g[1], v0h, v0l) - apply3(g21[...], v1h, v1l)
        for i, (v, vh, inv) in enumerate(((v0, v0h, s0), (v1, v1h, s1), (v2, v2.astype(BF16), s2))):
            part = (2.0 * v - vh.astype(F32)) * apply2(inv[...], vh)
            part = jnp.sum(part.reshape(BLOCK // SUB, SUB, span), axis=0)
            for j in range(span // LANES):
                totals[i] = totals[i] + part[:, j * LANES : (j + 1) * LANES]
        for r in range(max(0, n_tile - 2), n_tile):
            store(h, r).wait()
    for i in range(PICKS):
        loss[i] = jnp.sum(totals[i]) * (1.0 / (2.0 * BLOCK * cols))


VMEM = pl.BlockSpec(memory_space=pltpu.VMEM)
SMEM = pl.BlockSpec(memory_space=pltpu.SMEM)
ANY = pl.BlockSpec(memory_space=pl.ANY)
HBM = pl.BlockSpec(memory_space=pltpu.HBM)
def room(mib):
    return pltpu.CompilerParams(vmem_limit_bytes=mib << 20)


def shape(*dims, dtype=F32):
    return jax.ShapeDtypeStruct(dims, dtype)


def square(n):
    return shape(n, BLOCK, BLOCK)


HALVES = [pltpu.VMEM((HALF, HALF), F32), pltpu.VMEM((2, HALF, HALF), F32)]


def cost(us):
    return pl.CostEstimate(flops=int(us * 1e9), bytes_accessed=1 << 20, transcendentals=0)


def run_pack(n_row, picked, ids, src):
    local, cols = src.shape
    width = (BLOCK if picked else cols) // 2
    grain = min(BLOCK, local & -local)
    half = shape(BLOCK, width)
    return pl.pallas_call(
        functools.partial(pack_kernel, n_row, picked),
        out_shape=(shape(BLOCK, cols), half, half),
        in_specs=[SMEM, HBM],
        out_specs=(VMEM, VMEM, VMEM),
        scratch_shapes=[pltpu.SemaphoreType.DMA((1 + 2 * (BLOCK // grain),))],
        compiler_params=room(8),
        name="pack_panels" if picked else "pack_weights",
    )(ids, pltpu.with_memory_space_constraint(src, pltpu.HBM))


def run_first(n_row, local, ids, mine, other):
    return pl.pallas_call(
        functools.partial(first_kernel, n_row, local),
        out_shape=(shape(BLOCK, BLOCK), square(2), square(3)),
        in_specs=[SMEM, VMEM, VMEM],
        out_specs=(VMEM, VMEM, VMEM),
        scratch_shapes=[
            pltpu.VMEM((2, BLOCK, PICKS * BLOCK), F32),
            pltpu.VMEM((2, BLOCK, HALF), F32),
            pltpu.VMEM((PICKS, PICKS, BLOCK, BLOCK), F32),
        ]
        + HALVES,
        compiler_params=room(16),
        cost_estimate=cost(13),
        name="first_pick",
    )(ids, mine, other)


def run_second(a):
    one = shape(BLOCK, BLOCK)
    return pl.pallas_call(
        second_kernel,
        out_shape=(one, one, one),
        in_specs=[VMEM],
        out_specs=(VMEM,) * 3,
        scratch_shapes=HALVES,
        compiler_params=room(10),
        cost_estimate=cost(12),
        name="second_pick",
    )(a)


def run_third(*args):
    n = PICKS * BLOCK
    return pl.pallas_call(
        third_kernel,
        out_shape=(shape(BLOCK, BLOCK), shape(n, n)),
        in_specs=[VMEM] * 5,
        out_specs=(VMEM,) * 2,
        scratch_shapes=HALVES,
        compiler_params=room(14),
        cost_estimate=cost(14),
        name="third_pick",
    )(*args)


def tile_of(rows):
    return max(t for t in range(SUB, 2 * BLOCK + 1, SUB) if rows % t == 0)


def run_left(k, panels):
    rows, n = panels.shape
    tile = tile_of(rows)
    return pl.pallas_call(
        left_kernel,
        grid=(rows // tile,),
        out_shape=shape(rows, 2 * n, dtype=BF16),
        in_specs=[VMEM, pl.BlockSpec((tile, n), lambda i: (i, 0))],
        out_specs=pl.BlockSpec((tile, 2 * n), lambda i: (i, 0)),
        scratch_shapes=[pltpu.VMEM((3 * n, n), BF16)],
        compiler_params=room(24),
        cost_estimate=cost(10),
        name="left_factor",
    )(k, panels)


def run_final(n_row, ids, weights, t, zm, ym, zo, yo, m_mine, m_other, s0, s1, s2, g, g21):
    rows, cols = weights.shape
    n = PICKS * BLOCK
    n_z = zm.shape[0]
    return pl.pallas_call(
        functools.partial(final_kernel, n_row),
        out_shape=(shape(rows, cols), shape(PICKS)),
        in_specs=[SMEM, VMEM, VMEM] + [ANY] * 6 + [VMEM] * 5,
        out_specs=(ANY, SMEM),
        scratch_shapes=[
            pltpu.VMEM((n, cols), F32),
            pltpu.VMEM((2 * n, cols), BF16),
            pltpu.VMEM((n, cols), BF16),
            pltpu.VMEM((2, tile_of(rows), (cols // 2 + BLOCK - 1) // BLOCK * BLOCK), F32),
            pltpu.SemaphoreType.DMA((2, 6 * n_z)),
            pltpu.SemaphoreType.DMA((2,)),
        ],
        compiler_params=room(30),
        cost_estimate=cost(18),
        name="final_update",
    )(ids, weights, t, zm, ym, zo, yo, m_mine, m_other, s0, s1, s2, g, g21)


def body(n_row, panels, weights, block_ids):
    local, cols = weights.shape
    n_chip = n_row // 2
    s = BLOCK // n_chip
    idx = lax.axis_index("row")
    core, chip = idx & 1, idx >> 1
    last = n_row - 1

    def swap(x, bit):
        return lax.ppermute(x, "row", [(i, i ^ bit) for i in range(n_row)])

    def parts(x, bit_value):
        half = x.shape[0] // 2
        keep = lax.dynamic_slice_in_dim(x, bit_value * half, half, 0)
        return keep, lax.dynamic_slice_in_dim(x, (1 - bit_value) * half, half, 0)

    from_root = jnp.where(core == 0, chip, n_chip - 1 - chip)

    def scatter(x):
        bit = n_chip // 2
        while bit:
            keep, send = parts(x, (chip // bit) & 1)
            pairs = []
            for c in range(0, n_chip, 2 * bit):
                pairs += [(2 * c, 2 * (c + bit)), (last - 2 * c, last - 2 * (c + bit))]
            got = lax.ppermute(send, "row", pairs)
            x = jnp.where(from_root % (2 * bit) == bit, got, keep)
            bit //= 2
        return x

    def halve_core(keep, send):
        return (keep + swap(send, 1)).reshape(n_chip, s, keep.shape[1])

    def halve_step(x, bit):
        half = x.reshape(x.shape[0] // 2, 2, s, x.shape[2])
        mine = (chip // bit) & 1
        keep = lax.dynamic_index_in_dim(half, mine, 1, keepdims=False)
        send = lax.dynamic_index_in_dim(half, 1 - mine, 1, keepdims=False)
        return keep + swap(send, 2 * bit)

    def halve(x, bits):
        for bit in bits:
            x = halve_step(x, bit)
        return x

    tie = lax.optimization_barrier
    n_z = n_chip // 2
    bits = [1 << i for i in range(n_chip.bit_length() - 1)]

    a_block, a_keep, a_send = run_pack(n_row, True, block_ids, panels)
    a_mid = halve(halve_core(a_keep, a_send), bits)
    a_own = jnp.concatenate([scatter(a_block), a_mid.reshape(s, -1)], axis=1)

    w_block, w_keep, w_send = run_pack(n_row, False, block_ids, weights)
    w_mid = halve_core(w_keep, w_send)
    a_own, w_mid = tie((a_own, w_mid))
    w_line = scatter(w_block)
    a_mine = jnp.stack([a_own] + [swap(a_own, 2 * k) for k in range(1, n_chip)])
    w_mid = halve_step(w_mid, bits[0])
    a_mine, w_mid, w_line = tie((a_mine, w_mid, w_line))
    a_other = swap(a_mine, 1)
    w_mid = halve(w_mid, bits[1:-1])
    a_other, w_mid = tie((a_other, w_mid))

    f_z = [w_line] + [swap(w_line, 4 * k) for k in range(1, n_z)]
    w_mid = halve(w_mid, bits[-1:]).reshape(s, -1)
    s0, g, a1 = run_first(n_row, local, block_ids, a_mine, a_other)
    a1, w_mid = tie((a1, w_mid))
    m_y = swap(w_mid, 2)
    s1, g21, a2 = run_second(a1)
    a2, m_y, *f_z = tie((a2, m_y, *f_z))
    m_parts = jnp.stack([w_mid, m_y])
    m_z = [m_parts] + [swap(m_parts, 4 * k) for k in range(1, n_z)]
    zm = jnp.stack(f_z)
    ym = swap(zm, 2)
    zo = swap(zm, 1)
    s2, k = run_third(a2, s0, s1, g, g21)
    t = run_left(k, panels)
    t, ym, zo, *m_z = tie((t, ym, zo, *m_z))
    m_mine = jnp.concatenate(m_z, axis=0)
    m_other = swap(m_mine, 1)
    yo = swap(ym, 1)
    return run_final(n_row, block_ids, weights, t, zm, ym, zo, yo, m_mine, m_other, s0, s1, s2, g, g21)


def solution(mesh):
    n_row = mesh.shape["row"]
    rows = P(("groups", "row"), None)
    return jax.shard_map(
        functools.partial(body, n_row),
        mesh=mesh,
        in_specs=(rows, rows, P("groups")),
        out_specs=(rows, P("groups")),
        check_vma=False,
    )
```

```python
import functools

import jax
import jax.numpy as jnp
from jax import lax
from jax.experimental import pallas as pl
from jax.experimental.pallas import tpu as pltpu
from jax.sharding import PartitionSpec as P

BLOCK = 256
PICKS = 3
HALF = BLOCK // 2
SUB = 8
LANES = 128
EXACT = lax.Precision.HIGHEST
F32 = jnp.float32
BF16 = jnp.bfloat16


def mm(a, b):
    return lax.dot_general(a, b, (((1,), (0,)), ((), ())), precision=EXACT, preferred_element_type=F32)


def mm_nt(a, b):
    return lax.dot_general(a, b, (((1,), (1,)), ((), ())), precision=EXACT, preferred_element_type=F32)


def mm_tn(a, b):
    return lax.dot_general(a, b, (((0,), (0,)), ((), ())), precision=EXACT, preferred_element_type=F32)


def lane_bcast(x, c):
    return jnp.broadcast_to(x[:, c : c + 1], (SUB, LANES))


def row_bcast(x, j):
    return jnp.broadcast_to(x[j : j + 1, :], (SUB, LANES))


def inv_half(m):
    n_panels = HALF // SUB
    rows = [m[SUB * i : SUB * i + SUB, :] for i in range(n_panels)]
    lane = lax.broadcasted_iota(jnp.int32, (SUB, LANES), 1)
    sub = lax.broadcasted_iota(jnp.int32, (SUB, LANES), 0)
    for p in range(n_panels):
        panel = rows[p]
        cols = [lane_bcast(panel, SUB * p + k) for k in range(SUB)]
        for j in range(SUB):
            is_j = sub == j
            r = 1.0 / row_bcast(cols[j], j)
            f = cols[j] * r
            panel = jnp.where(lane == SUB * p + j, jnp.where(is_j, 1.0, 0.0), panel)
            u = row_bcast(panel, j)
            panel = jnp.where(is_j, u * r, panel - f * u)
            for k in range(j + 1, SUB):
                uk = row_bcast(cols[k], j)
                cols[k] = jnp.where(is_j, uk * r, cols[k] - f * uk)
        reps = [row_bcast(panel, k) for k in range(SUB)]
        in_panel = (lane >= SUB * p) & (lane < SUB * p + SUB)
        for step in range(1, n_panels):
            i = (p + step) % n_panels
            t = [lane_bcast(rows[i], SUB * p + k) * reps[k] for k in range(SUB)]
            total = ((t[0] + t[1]) + (t[2] + t[3])) + ((t[4] + t[5]) + (t[6] + t[7]))
            rows[i] = jnp.where(in_panel, 0.0, rows[i]) - total
        rows[p] = panel
    return jnp.concatenate(rows, axis=0)


def inv_block(ref, half_in, half_out):
    def one(h, _):
        @pl.when(h == 0)
        def _():
            half_in[...] = ref[:HALF, :HALF]

        @pl.when(h == 1)
        def _():
            c = ref[HALF:, :HALF]
            half_in[...] = ref[HALF:, HALF:] - mm_nt(mm(c, half_out[0]), c)

        half_out[h] = inv_half(half_in[...])
        return 0

    lax.fori_loop(0, 2, one, 0)
    ai, si = half_out[0], half_out[1]
    g = mm(ref[HALF:, :HALF], ai)
    h = mm(si, g)
    top = jnp.concatenate([ai + mm_tn(g, h), -h.T], axis=1)
    return jnp.concatenate([top, jnp.concatenate([-h, si], axis=1)], axis=0)


def split(x):
    hi = x.astype(BF16)
    return hi, (x - hi.astype(F32)).astype(BF16)


def dot3k(stacked_left, stacked_right):
    return jnp.dot(stacked_left, stacked_right, preferred_element_type=F32)


def left3(x):
    hi, lo = split(x)
    return jnp.concatenate([hi, hi, lo], axis=1)


def right3(x):
    hi, lo = split(x)
    return jnp.concatenate([hi, lo, hi], axis=0)


def apply2(left, right):
    both = jnp.dot(jnp.concatenate(split(left), axis=0), right, preferred_element_type=F32)
    return both[:BLOCK] + both[BLOCK:]


def apply3(left, right_hi, right_lo):
    return apply2(left, right_hi) + jnp.dot(left.astype(BF16), right_lo, preferred_element_type=F32)


def positions(n_row, local, ids):
    last_block = n_row * local // BLOCK - 1
    at = lambda v: jnp.where(ids[0] == v, 0, jnp.where(ids[1] == v, 1, 2)).astype(jnp.int32)
    c_f, c_l = at(0), at(last_block)
    return c_f, c_l, PICKS - c_f - c_l, ids[0] + ids[1] + ids[2] - last_block


def pack_kernel(n_row, picked, ids, src, line_out, keep_out, send_out, sems):
    local, cols = src.shape
    idx = lax.axis_index("row")
    core = idx & 1
    _, _, c_m, mid = positions(n_row, local, ids)
    grain = min(BLOCK, local & -local)
    width = keep_out.shape[1]
    base = jnp.where(idx == n_row - 1, local - BLOCK, 0)
    line = pltpu.make_async_copy(src.at[pl.ds(pl.multiple_of(base, SUB), BLOCK), :], line_out, sems.at[0])
    line.start()
    left = c_m * BLOCK if picked else 0

    def copy(i, out, side, sem):
        row = pl.multiple_of(mid * BLOCK + i * grain - idx * local, SUB)
        at = src.at[pl.ds(row, grain), pl.ds(pl.multiple_of(left + side * width, LANES), width)]
        return pltpu.make_async_copy(at, out.at[pl.ds(i * grain, grain), :], sem)

    def each(act):
        for i in range(BLOCK // grain):
            row = mid * BLOCK + i * grain - idx * local
            owned = (row >= 0) & (row < local)
            for j, (out, side) in enumerate(((keep_out, core), (send_out, 1 - core))):
                act(i, out, side, sems.at[1 + 2 * i + j], owned)

    def begin(i, out, side, sem, owned):
        @pl.when(owned)
        def _():
            copy(i, out, side, sem).start()

        @pl.when(jnp.logical_not(owned))
        def _():
            out[i * grain : (i + 1) * grain, :] = jnp.zeros((grain, width), F32)

    def finish(i, out, side, sem, owned):
        @pl.when(owned)
        def _():
            copy(i, out, side, sem).wait()

    each(begin)
    each(finish)
    line.wait()


def first_kernel(n_row, local, ids, mine, other, s_out, g_out, a_out, fl, mid, blk, half_in, half_out):
    idx = lax.axis_index("row")
    core, chip = idx % 2, idx // 2
    c_f, c_l, c_m, _ = positions(n_row, local, ids)
    n_chip, s = mine.shape[0], mine.shape[1]
    width = PICKS * BLOCK
    for k in range(n_chip):
        row = pl.multiple_of((chip ^ k) * s, SUB)
        fl[core, pl.ds(row, s), :] = mine[k, :, :width]
        mid[core, pl.ds(row, s), :] = mine[k, :, width:]
        fl[1 - core, pl.ds(row, s), :] = other[k, :, :width]
        mid[1 - core, pl.ds(row, s), :] = other[k, :, width:]
    for j in range(PICKS):
        blk[c_f, j] = fl[0, :, j * BLOCK : (j + 1) * BLOCK]
        blk[c_l, j] = fl[1, :, j * BLOCK : (j + 1) * BLOCK]
    blk[c_m, c_f] = blk[c_f, c_m].T
    blk[c_m, c_l] = blk[c_l, c_m].T
    blk[c_m, c_m, :, :HALF] = mid[0]
    blk[c_m, c_m, :, HALF:] = mid[1]
    s0 = inv_block(blk.at[0, 0], half_in, half_out)
    s_out[...] = s0
    a10, a20 = blk[1, 0], blk[2, 0]
    g10, g20 = mm(a10, s0), mm(a20, s0)
    g_out[0] = g10
    g_out[1] = g20
    a_out[0] = blk[1, 1] - mm_nt(g10, a10)
    a_out[1] = blk[2, 1] - mm_nt(g20, a10)
    a_out[2] = blk[2, 2] - mm_nt(g20, a20)


def second_kernel(a_in, s_out, g_out, a_out, half_in, half_out):
    s1 = inv_block(a_in.at[0], half_in, half_out)
    s_out[...] = s1
    a21 = a_in[1]
    g21 = mm(a21, s1)
    g_out[...] = g21
    a_out[...] = a_in[2] - mm_nt(g21, a21)


def third_kernel(a_in, s0, s1, g, g21, s_out, k_out, half_in, half_out):
    s2 = inv_block(a_in, half_in, half_out)
    s_out[...] = s2
    g10, g20 = g[0], g[1]
    j21 = -g21[...]
    j20 = mm(g21[...], g10) - g20
    k21, k20 = mm(s2, j21), mm(s2, j20)
    t10 = mm(s1[...], g10)
    k11 = s1[...] + mm_tn(j21, k21)
    k10 = mm_tn(j21, k20) - t10
    k00 = s0[...] + mm_tn(g10, t10) + mm_tn(j20, k20)
    e = lambda i: slice(i * BLOCK, (i + 1) * BLOCK)
    k_out[e(2), e(2)] = s2
    k_out[e(2), e(1)] = k21
    k_out[e(1), e(2)] = k21.T
    k_out[e(2), e(0)] = k20
    k_out[e(0), e(2)] = k20.T
    k_out[e(1), e(1)] = k11
    k_out[e(1), e(0)] = k10
    k_out[e(0), e(1)] = k10.T
    k_out[e(0), e(0)] = k00


def left_kernel(k_ref, p_ref, out, k3):
    @pl.when(pl.program_id(0) == 0)
    def _():
        k3[...] = right3(k_ref[...])

    n = p_ref.shape[1]
    hi, lo = split(dot3k(left3(p_ref[...]), k3[...]))
    out[:, :n] = hi
    out[:, n:] = lo


def final_kernel(n_row, ids, w_ref, t_ref, zm, ym, zo, yo, m_mine, m_other, s0, s1, s2, g, g21, out, loss, ws, hi, lo, obuf, in_sems, out_sems):
    local, cols = w_ref.shape
    n_z, s = zm.shape[0], zm.shape[1]
    width = cols // 2
    tile = obuf.shape[1]
    n_tile = local // tile
    idx = lax.axis_index("row")
    core, chip = idx & 1, idx >> 1
    c_f, c_l, c_m, mid_block = positions(n_row, local, ids)
    n = PICKS * BLOCK
    first = min(cols, (width + BLOCK - 1) // BLOCK * BLOCK)
    chunks = (slice(0, first), slice(first, cols))
    mine_at = jnp.where(core == 0, c_f, c_l) * BLOCK
    other_at = jnp.where(core == 0, c_l, c_f) * BLOCK

    def line_copies(cs):
        made = []
        for k in range(n_z):
            for j, (y, at, ref) in enumerate(((0, mine_at, zm), (1, mine_at, ym), (0, other_at, zo), (1, other_at, yo))):
                row = pl.multiple_of(at + (chip ^ (2 * k + y)) * s, SUB)
                sem = in_sems.at[0 if cs.start == 0 else 1, 4 * k + j]
                made.append(pltpu.make_async_copy(ref.at[k, :, cs], ws.at[pl.ds(row, s), cs], sem))
        return made

    def mid_copies(side, ref):
        made = []
        for k in range(2 * n_z):
            row = pl.multiple_of(c_m * BLOCK + (chip ^ k) * s, SUB)
            dst = ws.at[pl.ds(row, s), slice(side * width, (side + 1) * width)]
            made.append(pltpu.make_async_copy(ref.at[k], dst, in_sems.at[side, 4 * n_z + k]))
        return made

    for side in range(2):
        for owner, ref in ((0, m_mine), (1, m_other)):

            @pl.when((core ^ side) == owner)
            def _():
                for c in mid_copies(side, ref):
                    c.start()

        for c in line_copies(chunks[side]):
            c.start()

    def store(h, r):
        cs = chunks[h]
        slot = r & 1
        row = r * tile if isinstance(r, int) else pl.multiple_of(r * tile, SUB)
        src = obuf.at[slot, :, slice(0, cs.stop - cs.start)]
        return pltpu.make_async_copy(src, out.at[pl.ds(row, tile), cs], out_sems.at[slot])

    totals = [jnp.zeros((SUB, LANES), F32) for _ in range(PICKS)]
    e = lambda i: slice(i * BLOCK, (i + 1) * BLOCK)
    for h, cs in enumerate(chunks):
        span = cs.stop - cs.start
        if h == 0:
            for side in range(2):
                for c in mid_copies(side, m_mine):
                    c.wait()
        for c in line_copies(cs):
            c.wait()
        top, low = split(ws[:, cs])
        hi[:n, cs] = top
        hi[n:, cs] = top
        lo[:, cs] = low

        def one_tile(r, _):
            rs = pl.ds(pl.multiple_of(r * tile, 2 * SUB), tile)
            prod = jnp.dot(t_ref[rs, :], hi[:, cs], preferred_element_type=F32)
            prod = prod + jnp.dot(t_ref[rs, :n], lo[:, cs], preferred_element_type=F32)

            @pl.when(r >= 2)
            def _():
                store(h, r - 2).wait()

            block_of = (idx * local + r * tile + lax.broadcasted_iota(jnp.int32, (tile, 1), 0)) // BLOCK
            listed = (block_of == 0) | (block_of == n_row * local // BLOCK - 1) | (block_of == mid_block)
            obuf[r & 1, :, :span] = jnp.where(listed, 0.0, w_ref[rs, cs] - prod)
            store(h, r).start()
            return 0

        lax.fori_loop(0, n_tile, one_tile, 0)

        v0, v0h, v0l = ws[e(0), cs], hi[e(0), cs], lo[e(0), cs]
        v1 = ws[e(1), cs] - apply3(g[0], v0h, v0l)
        v1h, v1l = split(v1)
        v2 = ws[e(2), cs] - apply3(g[1], v0h, v0l) - apply3(g21[...], v1h, v1l)
        for i, (v, vh, inv) in enumerate(((v0, v0h, s0), (v1, v1h, s1), (v2, v2.astype(BF16), s2))):
            part = (2.0 * v - vh.astype(F32)) * apply2(inv[...], vh)
            part = jnp.sum(part.reshape(BLOCK // SUB, SUB, span), axis=0)
            for j in range(span // LANES):
                totals[i] = totals[i] + part[:, j * LANES : (j + 1) * LANES]
        for r in range(max(0, n_tile - 2), n_tile):
            store(h, r).wait()
    for i in range(PICKS):
        loss[i] = jnp.sum(totals[i]) * (1.0 / (2.0 * BLOCK * cols))


VMEM = pl.BlockSpec(memory_space=pltpu.VMEM)
SMEM = pl.BlockSpec(memory_space=pltpu.SMEM)
ANY = pl.BlockSpec(memory_space=pl.ANY)
HBM = pl.BlockSpec(memory_space=pltpu.HBM)
def room(mib):
    return pltpu.CompilerParams(vmem_limit_bytes=mib << 20)


def shape(*dims, dtype=F32):
    return jax.ShapeDtypeStruct(dims, dtype)


def square(n):
    return shape(n, BLOCK, BLOCK)


HALVES = [pltpu.VMEM((HALF, HALF), F32), pltpu.VMEM((2, HALF, HALF), F32)]


def cost(us):
    return pl.CostEstimate(flops=int(us * 1e9), bytes_accessed=1 << 20, transcendentals=0)


def run_pack(n_row, picked, ids, src):
    local, cols = src.shape
    width = (BLOCK if picked else cols) // 2
    grain = min(BLOCK, local & -local)
    half = shape(BLOCK, width)
    return pl.pallas_call(
        functools.partial(pack_kernel, n_row, picked),
        out_shape=(shape(BLOCK, cols), half, half),
        in_specs=[SMEM, HBM],
        out_specs=(VMEM, VMEM, VMEM),
        scratch_shapes=[pltpu.SemaphoreType.DMA((1 + 2 * (BLOCK // grain),))],
        compiler_params=room(8),
        name="pack_panels" if picked else "pack_weights",
    )(ids, pltpu.with_memory_space_constraint(src, pltpu.HBM))


def run_first(n_row, local, ids, mine, other):
    return pl.pallas_call(
        functools.partial(first_kernel, n_row, local),
        out_shape=(shape(BLOCK, BLOCK), square(2), square(3)),
        in_specs=[SMEM, VMEM, VMEM],
        out_specs=(VMEM, VMEM, VMEM),
        scratch_shapes=[
            pltpu.VMEM((2, BLOCK, PICKS * BLOCK), F32),
            pltpu.VMEM((2, BLOCK, HALF), F32),
            pltpu.VMEM((PICKS, PICKS, BLOCK, BLOCK), F32),
        ]
        + HALVES,
        compiler_params=room(16),
        cost_estimate=cost(13),
        name="first_pick",
    )(ids, mine, other)


def run_second(a):
    one = shape(BLOCK, BLOCK)
    return pl.pallas_call(
        second_kernel,
        out_shape=(one, one, one),
        in_specs=[VMEM],
        out_specs=(VMEM,) * 3,
        scratch_shapes=HALVES,
        compiler_params=room(10),
        cost_estimate=cost(12),
        name="second_pick",
    )(a)


def run_third(*args):
    n = PICKS * BLOCK
    return pl.pallas_call(
        third_kernel,
        out_shape=(shape(BLOCK, BLOCK), shape(n, n)),
        in_specs=[VMEM] * 5,
        out_specs=(VMEM,) * 2,
        scratch_shapes=HALVES,
        compiler_params=room(14),
        cost_estimate=cost(14),
        name="third_pick",
    )(*args)


def tile_of(rows):
    return max(t for t in range(SUB, 2 * BLOCK + 1, SUB) if rows % t == 0)


def run_left(k, panels):
    rows, n = panels.shape
    tile = tile_of(rows)
    return pl.pallas_call(
        left_kernel,
        grid=(rows // tile,),
        out_shape=shape(rows, 2 * n, dtype=BF16),
        in_specs=[VMEM, pl.BlockSpec((tile, n), lambda i: (i, 0))],
        out_specs=pl.BlockSpec((tile, 2 * n), lambda i: (i, 0)),
        scratch_shapes=[pltpu.VMEM((3 * n, n), BF16)],
        compiler_params=room(24),
        cost_estimate=cost(10),
        name="left_factor",
    )(k, panels)


def run_final(n_row, ids, weights, t, zm, ym, zo, yo, m_mine, m_other, s0, s1, s2, g, g21):
    rows, cols = weights.shape
    n = PICKS * BLOCK
    n_z = zm.shape[0]
    return pl.pallas_call(
        functools.partial(final_kernel, n_row),
        out_shape=(shape(rows, cols), shape(PICKS)),
        in_specs=[SMEM, VMEM, VMEM] + [ANY] * 6 + [VMEM] * 5,
        out_specs=(ANY, SMEM),
        scratch_shapes=[
            pltpu.VMEM((n, cols), F32),
            pltpu.VMEM((2 * n, cols), BF16),
            pltpu.VMEM((n, cols), BF16),
            pltpu.VMEM((2, tile_of(rows), (cols // 2 + BLOCK - 1) // BLOCK * BLOCK), F32),
            pltpu.SemaphoreType.DMA((2, 6 * n_z)),
            pltpu.SemaphoreType.DMA((2,)),
        ],
        compiler_params=room(30),
        cost_estimate=cost(18),
        name="final_update",
    )(ids, weights, t, zm, ym, zo, yo, m_mine, m_other, s0, s1, s2, g, g21)


def body(n_row, panels, weights, block_ids):
    local, cols = weights.shape
    n_chip = n_row // 2
    s = BLOCK // n_chip
    idx = lax.axis_index("row")
    core, chip = idx & 1, idx >> 1
    last = n_row - 1

    def swap(x, bit):
        return lax.ppermute(x, "row", [(i, i ^ bit) for i in range(n_row)])

    def parts(x, bit_value):
        half = x.shape[0] // 2
        keep = lax.dynamic_slice_in_dim(x, bit_value * half, half, 0)
        return keep, lax.dynamic_slice_in_dim(x, (1 - bit_value) * half, half, 0)

    from_root = jnp.where(core == 0, chip, n_chip - 1 - chip)

    def scatter(x):
        bit = n_chip // 2
        while bit:
            keep, send = parts(x, (chip // bit) & 1)
            pairs = []
            for c in range(0, n_chip, 2 * bit):
                pairs += [(2 * c, 2 * (c + bit)), (last - 2 * c, last - 2 * (c + bit))]
            got = lax.ppermute(send, "row", pairs)
            x = jnp.where(from_root % (2 * bit) == bit, got, keep)
            bit //= 2
        return x

    def halve_core(keep, send):
        return (keep + swap(send, 1)).reshape(n_chip, s, keep.shape[1])

    def halve_step(x, bit):
        half = x.reshape(x.shape[0] // 2, 2, s, x.shape[2])
        mine = (chip // bit) & 1
        keep = lax.dynamic_index_in_dim(half, mine, 1, keepdims=False)
        send = lax.dynamic_index_in_dim(half, 1 - mine, 1, keepdims=False)
        return keep + swap(send, 2 * bit)

    def halve(x, bits):
        for bit in bits:
            x = halve_step(x, bit)
        return x

    tie = lax.optimization_barrier
    n_z = n_chip // 2
    bits = [1 << i for i in range(n_chip.bit_length() - 1)]

    a_block, a_keep, a_send = run_pack(n_row, True, block_ids, panels)
    a_mid = halve(halve_core(a_keep, a_send), bits)
    a_own = jnp.concatenate([scatter(a_block), a_mid.reshape(s, -1)], axis=1)

    w_block, w_keep, w_send = run_pack(n_row, False, block_ids, weights)
    w_mid = halve_core(w_keep, w_send)
    a_own, w_mid = tie((a_own, w_mid))
    w_line = scatter(w_block)
    a_mine = jnp.stack([a_own] + [swap(a_own, 2 * k) for k in range(1, n_chip)])
    w_mid = halve_step(w_mid, bits[0])
    a_mine, w_mid = tie((a_mine, w_mid))
    a_other = swap(a_mine, 1)
    w_mid = halve(w_mid, bits[1:-1])
    a_other, w_mid = tie((a_other, w_mid))

    f_z = [w_line] + [swap(w_line, 4 * k) for k in range(1, n_z)]
    w_mid = halve(w_mid, bits[-1:]).reshape(s, -1)
    s0, g, a1 = run_first(n_row, local, block_ids, a_mine, a_other)
    a1, w_mid = tie((a1, w_mid))
    m_y = swap(w_mid, 2)
    s1, g21, a2 = run_second(a1)
    a2, m_y, *f_z = tie((a2, m_y, *f_z))
    m_parts = jnp.stack([w_mid, m_y])
    m_z = [m_parts] + [swap(m_parts, 4 * k) for k in range(1, n_z)]
    zm = jnp.stack(f_z)
    ym = swap(zm, 2)
    zo = swap(zm, 1)
    s2, k = run_third(a2, s0, s1, g, g21)
    t = run_left(k, panels)
    t, ym, zo, *m_z = tie((t, ym, zo, *m_z))
    m_mine = jnp.concatenate(m_z, axis=0)
    m_other = swap(m_mine, 1)
    yo = swap(ym, 1)
    return run_final(n_row, block_ids, weights, t, zm, ym, zo, yo, m_mine, m_other, s0, s1, s2, g, g21)


def solution(mesh):
    n_row = mesh.shape["row"]
    rows = P(("groups", "row"), None)
    return jax.shard_map(
        functools.partial(body, n_row),
        mesh=mesh,
        in_specs=(rows, rows, P("groups")),
        out_specs=(rows, P("groups")),
        check_vma=False,
    )
```
